128 devices in a mesh: ends: 2 (over z_hi), dp: 8 (over y, core), tp: 8 (over z_lo, x).
Axes of the slice: x: 4, y: 4, z: 4 (z_hi: 2, z_lo: 2; z = z_hi * 2 + z_lo), core: 2. Of those that a mesh axis runs over, the one named last changes fastest.
Arguments:
- grad: bfloat16 [2, 8, 16384, 3072], P('ends', 'dp', 'tp'), may hold values from -1800 to 1800
- master: float32 [8, 2048, 3072], P('tp', ('ends', 'dp')), may hold values from -3 to 3
- moment: float32 [8, 2048, 3072], P('tp', ('ends', 'dp')), may hold values from -3 to 3
- second: float32 [8, 2048, 3072], P('tp', ('ends', 'dp')), may hold values from 0.01 to 1
Outputs:
- weights: bfloat16 [16384, 3072], P('tp')
- master_out: float32 [8, 2048, 3072], P('tp', ('ends', 'dp'))
- moment_out: float32 [8, 2048, 3072], P('tp', ('ends', 'dp'))
- second_out: float32 [8, 2048, 3072], P('tp', ('ends', 'dp'))
The draws below stay inside these ranges and needn't reach their ends.
All inputs are finite; a program needn't handle non-finite values.
Results may differ from the reference program's by a relative error of at most 0.0034.
Values may be sent and summed in bfloat16 or wider, within the bound.
No kernel may reach another device: no remote copies, remote signals or barrier semaphores. Data moves between devices by JAX's collectives and lax.ppermute only.
A program may use at most 128 MiB of HBM per device.

```python
import math
import jax
import jax.numpy as jnp
from jax import lax

D = 3072
STEP = 10
ROWS_TP = 2048
VOCAB = 16384
N_ENDS = 2
N_DP = 8
N_TP = 8


def draw_grad(key, part):
    keys = jax.random.split(jax.random.fold_in(key, 17), 4)
    shape = (N_ENDS, N_DP, VOCAB, D)
    base = jax.random.truncated_normal(keys[0], -4.0, 4.0, shape, jnp.float32)
    members = N_ENDS * N_DP
    member = 0.5 * 3.0 ** (jnp.arange(members, dtype=jnp.float32) / max(members - 1, 1))
    member = member.reshape(N_ENDS, N_DP, 1, 1)
    position = (jnp.arange(VOCAB, dtype=jnp.int32) % ROWS_TP).astype(jnp.float32) / ROWS_TP
    rough = jnp.exp(jax.random.uniform(keys[2], (VOCAB,), jnp.float32, 0.0, math.log(10.0)))
    row_scale = 3.0 ** position * rough
    col_scale = jnp.exp(jax.random.uniform(keys[3], (D,), jnp.float32, 0.0, math.log(10.0)))
    values = base * member * row_scale[None, None, :, None] * col_scale[None, None, None, :]
    return values.astype(jnp.bfloat16)


def block_scale(stream_key, extent, shards, low, largest):
    gain, own = 1.0, jax.random.fold_in(stream_key, 6)
    for axis_at, parts in shards:
        draws = jnp.exp(jax.random.uniform(jax.random.fold_in(own, axis_at), (parts,), jnp.float32, low / len(shards), largest / len(shards)))
        gain = gain * jnp.repeat(draws, extent[axis_at] // parts).reshape([-1 if axis == axis_at else 1 for axis in range(len(extent))])
    return gain


def scatter_about(key, extent, deviation, most, pieces=(), held_as=jnp.bfloat16):
    result = jax.random.normal(key, extent, jnp.float32) * deviation
    if len(pieces) > 0:
        result = block_scale(key, extent, pieces, -0.22, 0.18) * result
    return jnp.clip(result, min=-most, max=most).astype(held_as)


def setup_inputs(seed: int = 0) -> dict:
    streams_of = jax.random.split(jax.random.key(seed), 5)
    return {
        "grad": draw_grad(jax.random.fold_in(streams_of[4], 71), 0),
        "master": scatter_about(streams_of[1], (N_TP, ROWS_TP, D), 0.5, 3.0, ((0, 8), (1, 16)), jnp.float32),
        "moment": scatter_about(streams_of[2], (N_TP, ROWS_TP, D), 0.5, 3.0, ((0, 8), (1, 16)), jnp.float32),
        "second": jnp.clip(jnp.exp(math.log(1.0) - 4.6051702 * jax.random.uniform(streams_of[3], (N_TP, ROWS_TP, D), jnp.float32) ** block_scale(streams_of[3], (N_TP, ROWS_TP, D), ((0, 8), (1, 16)), -0.2, 0.2)), 0.01, 1.0),
    }


def reference(grad, master, moment, second):
    stacked = grad.reshape(N_ENDS * N_DP, VOCAB, D)

    def accumulate(carry, member):
        return (carry + member.astype(jnp.float32), None)
    summed, _ = lax.scan(accumulate, jnp.zeros((VOCAB, D), jnp.float32), stacked)
    norm = jnp.sqrt(jnp.sum(summed * summed))
    factor = jnp.minimum(jnp.float32(1.0), jnp.sqrt(jnp.float32(VOCAB * D)) / (norm + 1e-06))
    clipped = (factor * summed).reshape(N_TP, ROWS_TP, D)
    moment_out = 0.9 * moment + 0.1 * clipped
    second_out = 0.999 * second + 0.001 * clipped * clipped
    update = moment_out / (1.0 - 0.9 ** STEP) / (jnp.sqrt(second_out / (1.0 - 0.999 ** STEP)) + 1e-08)
    master_out = master - 0.01 * (update + 0.1 * master)
    weights = master_out.reshape(VOCAB, D).astype(jnp.bfloat16)
    return (weights, master_out, moment_out, second_out)
```

```python
import jax
import jax.numpy as jnp
from jax import lax
from jax.experimental import pallas as pl
from jax.experimental.pallas import tpu as pltpu
from jax.sharding import Mesh
from jax.sharding import PartitionSpec as P

STEP = 10
ENDS_DP = ("ends", "dp_0", "dp_1")
TP = ("tp_0", "tp_1")
DP = ("dp_0", "dp_1")

SIZE = (32, 32, 32, 32)
START = (0, 32, 64, 96)
P1, P3, Z = "p1", "p3", "z"


def over(link, seg):
    de, dy, q = seg
    if link == P1:
        return (de, dy ^ 1, q)
    if link == P3:
        return (de, dy ^ 3, q)
    return (de ^ 1, dy, q)


REDUCE = (
    {
        Z: ((1, 2, 1), (1, 1, 1), (1, 2, 2), (1, 3, 2)),
        P1: ((1, 2, 0), (0, 2, 0), (1, 1, 0), (0, 1, 0)),
        P3: ((1, 2, 3), (0, 2, 3), (1, 3, 3), (0, 3, 3)),
    },
    {
        Z: ((1, 0, 1), (1, 0, 2), (1, 3, 1), (1, 1, 2)),
        P1: ((1, 1, 3), (0, 1, 3), (0, 2, 1), (0, 1, 1)),
        P3: ((1, 3, 0), (0, 3, 0), (0, 2, 2), (0, 3, 2)),
    },
    {
        Z: ((1, 0, 0), (1, 0, 3)),
        P1: ((0, 1, 2),),
        P3: ((0, 3, 1),),
    },
)
OWN = tuple((0, 0, q) for q in range(4))
GATHER = (
    {
        Z: ((0, 3, 1), (0, 1, 1), (0, 1, 2), (0, 3, 2)),
        P1: ((1, 0, 0), (0, 3, 0), (1, 0, 3), (0, 3, 1)),
        P3: ((1, 0, 3), (0, 1, 3), (1, 0, 0), (0, 1, 2)),
    },
    {
        Z: ((0, 2, 1), (0, 2, 2)),
        P1: ((1, 3, 0),),
        P3: ((1, 1, 3),),
    },
)


def send(link, x):
    if link == Z:
        return lax.ppermute(x, "ends", [(0, 1), (1, 0)])
    flip = 1 if link == P1 else 3
    return lax.ppermute(x, "dp_0", [(i, i ^ flip) for i in range(4)])


def to_other_core(x):
    return lax.ppermute(x, "dp_1", [(0, 1), (1, 0)])


def rows_of(segs):
    return sum(SIZE[q] for _, _, q in segs)


def layout(segs):
    at, row = {}, 0
    for seg in segs:
        at[seg] = row
        row += SIZE[seg[2]]
    return at


def slot(de, dy, other):
    return (de * 4 + dy) * 2 + other


def row_at(table, place):
    if isinstance(place, int):
        return place
    block, q = place
    return pl.multiple_of(table[block] * 128 + START[q], 8)


class Build:
    def __init__(self):
        self.arrays, self.outs, self.work = [], [], []

    def array(self, x):
        for i, have in enumerate(self.arrays):
            if have is x:
                return i
        self.arrays.append(x)
        return len(self.arrays) - 1

    def out(self, rows, dtype=jnp.bfloat16):
        self.outs.append((rows, dtype))
        return len(self.outs) - 1

    def piece(self, out, place, rows, sources):
        self.work.append((out, place, rows, [(self.array(x), at) for x, at in sources]))

    def run(self, table, into=None, squares=False):
        width = self.arrays[0].shape[-1]
        work, n_in, n_out = self.work, len(self.arrays), len(self.outs)
        loads = []
        for out, place, rows, sources in work:
            if len(sources) > 1 or squares:
                loads.extend((x, at, rows) for x, at in sources)
        sums = [w for w in work if len(w[3]) > 1 or squares]
        deepest = max([w[2] for w in work])

        def kernel(table_ref, *refs):
            ins, refs = refs[:n_in], refs[n_in:]
            if into is not None:
                refs = refs[1:]
            outs, refs = refs[:n_out], refs[n_out:]
            if squares:
                square_ref, refs = refs[0], refs[1:]
            (in_buf, in_sem, out_sem), bufs = refs[:3], refs[3:]

            def load(k):
                x, at, rows = loads[k]
                return pltpu.make_async_copy(
                    ins[x].at[pl.ds(row_at(table_ref, at), rows)],
                    in_buf.at[k, pl.ds(0, rows)],
                    in_sem.at[k],
                )

            for k in range(len(loads)):
                load(k).start()
            started, k, s = [], 0, 0
            total = None
            for w, (out, place, rows, sources) in enumerate(work):
                target = outs[out].at[pl.ds(row_at(table_ref, place), rows)]
                if len(sources) == 1 and not squares:
                    x, at = sources[0]
                    copy = pltpu.make_async_copy(
                        ins[x].at[pl.ds(row_at(table_ref, at), rows)], target, out_sem.at[w]
                    )
                    copy.start()
                    started.append(copy)
            for w, (out, place, rows, sources) in enumerate(work):
                if len(sources) == 1 and not squares:
                    continue
                target = outs[out].at[pl.ds(row_at(table_ref, place), rows)]
                acc = None
                for _ in sources:
                    load(k).wait()
                    term = in_buf[k, pl.ds(0, rows)].astype(jnp.float32)
                    acc = term if acc is None else acc + term
                    k += 1
                if squares:
                    part = jnp.sum((acc * acc).reshape(rows // 8, 8, width // 128, 128), axis=(0, 2))
                    total = part if total is None else total + part
                bufs[0][s, pl.ds(0, rows)] = acc.astype(bufs[0].dtype)
                copy = pltpu.make_async_copy(bufs[0].at[s, pl.ds(0, rows)], target, out_sem.at[w])
                copy.start()
                started.append(copy)
                s += 1
            if squares:
                square_ref[...] = total
            for copy in started:
                copy.wait()

        out_dtype = self.outs[0][1]
        out_shape = [jax.ShapeDtypeStruct((rows, width), dtype) for rows, dtype in self.outs]
        out_specs = [pl.BlockSpec(memory_space=pl.ANY)] * n_out
        if squares:
            out_shape.append(jax.ShapeDtypeStruct((8, 128), jnp.float32))
            out_specs.append(pl.BlockSpec(memory_space=pltpu.VMEM))
        scratch = [
            pltpu.VMEM((max(len(loads), 1), deepest if loads else 8, width), jnp.bfloat16),
            pltpu.SemaphoreType.DMA((max(len(loads), 1),)),
            pltpu.SemaphoreType.DMA((len(work),)),
        ]
        if sums:
            scratch.append(pltpu.VMEM((len(sums), deepest, width), out_dtype))
        moved = sum((len(w[3]) + 1) * w[2] for w in work) * width * 2
        extra = [] if into is None else [into]
        return pl.pallas_call(
            kernel,
            out_shape=out_shape,
            in_specs=[pl.BlockSpec(memory_space=pltpu.SMEM)]
            + [pl.BlockSpec(memory_space=pl.ANY)] * (n_in + len(extra)),
            out_specs=out_specs,
            scratch_shapes=scratch,
            input_output_aliases={} if into is None else {1 + n_in: 0},
            compiler_params=pltpu.CompilerParams(vmem_limit_bytes=40 * 2**20),
            cost_estimate=pl.CostEstimate(flops=0, bytes_accessed=moved, transcendentals=0),
        )(table, *self.arrays, *extra)


def reduce_rows(grad, table):
    plans = [{link: segs for link, segs in r.items()} for r in REDUCE]
    groups = [[seg for segs in plan.values() for seg in segs] for plan in plans[:2]]
    groups.append([seg for segs in plans[2].values() for seg in segs] + list(OWN))

    held = {}
    for group in groups:
        at = layout(group)
        build = Build()
        out = build.out(rows_of(group))
        for de, dy, q in group:
            build.piece(out, at[de, dy, q], SIZE[q], [(grad, (slot(de, dy, 1), q))])
        got = to_other_core(build.run(table)[0])
        for de, dy, q in group:
            held[de, dy, q] = [(grad, (slot(de, dy, 0), q)), (got, at[de, dy, q])]

    for plan in plans:
        build = Build()
        for link, segs in plan.items():
            at = layout(segs)
            out = build.out(rows_of(segs))
            for seg in segs:
                build.piece(out, at[seg], SIZE[seg[2]], held[seg])
        for (link, segs), x in zip(plan.items(), build.run(table)):
            at = layout(segs)
            got = send(link, x)
            for seg in segs:
                held[over(link, seg)].append((got, at[seg]))

    build = Build()
    out = build.out(128, jnp.float32)
    for seg in OWN:
        build.piece(out, START[seg[2]], SIZE[seg[2]], held[seg])
    return build.run(table, squares=True)


def gather_rows(own, table):
    held = {seg: (own, START[seg[2]]) for seg in OWN}
    out = None
    fresh = [(own, START, OWN)]
    for plan in ({link: OWN for link in (Z, P1, P3)},) + GATHER:
        if plan.keys() and all(segs == OWN for segs in plan.values()):
            messages = [own] * len(plan)
        else:
            build = Build()
            for link, segs in plan.items():
                at = layout(segs)
                to = build.out(rows_of(segs))
                for seg in segs:
                    build.piece(to, at[seg], SIZE[seg[2]], [held[seg]])
            messages = build.run(table)
        for (link, segs), x in zip(plan.items(), messages):
            at = layout(segs)
            got = send(link, x)
            fresh.append((got, at, tuple(segs), link))
            for seg in segs:
                held[over(link, seg)] = (got, at[seg])
        build = Build()
        build.out(2048)
        for x, at, segs, *link in fresh:
            other = to_other_core(x)
            for seg in segs:
                row = at[seg[2]] if not link else at[seg]
                de, dy, q = over(link[0], seg) if link else seg
                build.piece(0, (slot(de, dy, 0), q), SIZE[q], [(x, row)])
                build.piece(0, (slot(de, dy, 1), q), SIZE[q], [(other, row)])
        out = build.run(table, into=out)[0]
        fresh = []
    return out


def total_over_all(x):
    x = x + lax.ppermute(x, "dp_1", [(0, 1), (1, 0)])
    for axes in ("dp_0", "tp_1", ("ends", "tp_0")):
        for flip in (1, 3):
            x = x + lax.ppermute(x, axes, [(i, i ^ flip) for i in range(4)])
    return jnp.sum(x)


def per_device(grad, master, moment, second):
    rows_tp = grad.shape[2]
    width = grad.shape[3]
    e, y, c = (lax.axis_index(a) for a in ENDS_DP)
    table = jnp.stack(
        [
            ((e ^ de) * 4 + (y ^ dy)) * 2 + (c ^ other)
            for de in range(2)
            for dy in range(4)
            for other in range(2)
        ]
    ).astype(jnp.int32)
    summed, parts = reduce_rows(grad.reshape(rows_tp, width), table)
    squares = total_over_all(parts)
    vocab_total = rows_tp * lax.axis_size(TP)
    factor = jnp.minimum(
        jnp.float32(1.0), jnp.sqrt(jnp.float32(vocab_total * width)) / (jnp.sqrt(squares) + 1e-06)
    )
    clipped = factor * summed
    moment_out = 0.9 * moment[0] + 0.1 * clipped
    second_out = 0.999 * second[0] + 0.001 * clipped * clipped
    update = moment_out / (1.0 - 0.9**STEP) / (jnp.sqrt(second_out / (1.0 - 0.999**STEP)) + 1e-08)
    master_out = master[0] - 0.01 * (update + 0.1 * master[0])
    weights = gather_rows(master_out.astype(jnp.bfloat16), table)
    return (weights, master_out[None], moment_out[None], second_out[None])


def solution(mesh):
    finer = Mesh(
        mesh.devices.reshape(mesh.shape["ends"], 4, 2, 2, 4),
        ("ends", "dp_0", "dp_1", "tp_0", "tp_1"),
    )
    return jax.shard_map(
        per_device,
        mesh=finer,
        in_specs=(
            P("ends", DP, TP, None),
            P(TP, ENDS_DP, None),
            P(TP, ENDS_DP, None),
            P(TP, ENDS_DP, None),
        ),
        out_specs=(P(TP, None), P(TP, ENDS_DP, None), P(TP, ENDS_DP, None), P(TP, ENDS_DP, None)),
        check_vma=False,
    )
```

```python
import jax
import jax.numpy as jnp
from jax import lax
from jax.experimental import pallas as pl
from jax.experimental.pallas import tpu as pltpu
from jax.sharding import Mesh
from jax.sharding import PartitionSpec as P

STEP = 10
ENDS_DP = ("ends", "dp_0", "dp_1")
TP = ("tp_0", "tp_1")
DP = ("dp_0", "dp_1")

SIZE = (32, 32, 32, 32)
START = (0, 64, 96, 32)
STEP_COLUMNS = 512
P1, P3, Z = "p1", "p3", "z"


def over(link, seg):
    de, dy, q = seg
    if link == P1:
        return (de, dy ^ 1, q)
    if link == P3:
        return (de, dy ^ 3, q)
    return (de ^ 1, dy, q)


REDUCE = (
    {
        Z: ((1, 2, 1), (1, 1, 1), (1, 2, 2), (1, 3, 2)),
        P1: ((1, 2, 0), (0, 2, 0), (1, 1, 0), (0, 1, 0)),
        P3: ((1, 2, 3), (0, 2, 3), (1, 3, 3), (0, 3, 3)),
    },
    {
        Z: ((1, 0, 1), (1, 0, 2), (1, 3, 1), (1, 1, 2)),
        P1: ((1, 1, 3), (0, 1, 3), (0, 2, 1), (0, 1, 1)),
        P3: ((1, 3, 0), (0, 3, 0), (0, 2, 2), (0, 3, 2)),
    },
    {
        Z: ((1, 0, 0), (1, 0, 3)),
        P1: ((0, 1, 2),),
        P3: ((0, 3, 1),),
    },
)
CORE_PARTS = (
    (
        (
            (1, 2, 0, 128),
            (0, 2, 0, 64),
            (1, 1, 0, 32),
            (1, 1, 64, 32),
            (1, 3, 32, 32),
            (1, 3, 96, 32),
            (0, 1, 0, 32),
            (0, 3, 32, 32),
        ),
    ),
    (
        ((1, 1, 32, 32), (1, 1, 96, 32), (1, 3, 0, 32), (1, 3, 64, 32)),
        ((0, 1, 32, 64), (0, 2, 64, 64)),
        ((0, 3, 0, 32), (0, 3, 96, 32), (1, 0, 64, 64)),
        ((0, 1, 96, 32), (0, 3, 64, 32), (1, 0, 0, 64)),
        ((0, 0, 0, 128),),
    ),
)
OWN = ((0, 0, 0), (0, 0, 3), (0, 0, 1), (0, 0, 2))
GATHER = (
    {Z: OWN, P1: OWN, P3: OWN},
    {
        Z: ((0, 3, 1), (0, 1, 1), (0, 1, 2), (0, 3, 2)),
        P1: ((1, 0, 0), (1, 0, 3), (0, 3, 0), (0, 3, 1)),
        P3: ((1, 0, 0), (1, 0, 3), (0, 1, 3), (0, 1, 2)),
    },
    {
        Z: ((0, 2, 1), (0, 2, 2)),
        P1: ((1, 3, 0),),
        P3: ((1, 1, 3),),
    },
)


def send(link, x, name):
    with jax.named_scope(f"{name}_{link}"):
        return _send(link, x)


def _send(link, x):
    if link == Z:
        return lax.ppermute(x, "ends", [(0, 1), (1, 0)])
    flip = 1 if link == P1 else 3
    return lax.ppermute(x, "dp_0", [(i, i ^ flip) for i in range(4)])


def to_other_core(x, name):
    with jax.named_scope(f"{name}_core"):
        return lax.ppermute(x, "dp_1", [(0, 1), (1, 0)])


def rows_of(segs):
    return sum(SIZE[q] for _, _, q in segs)


def layout(segs):
    at, row = {}, 0
    for seg in segs:
        at[seg] = row
        row += SIZE[seg[2]]
    return at


def slot(de, dy, other):
    return (de * 4 + dy) * 2 + other


def block_row(table, block, row):
    return pl.multiple_of(table[block] * 128 + row, 8)


IN_VMEM = pl.BlockSpec(memory_space=pltpu.VMEM)
IN_HBM = pl.BlockSpec(memory_space=pltpu.HBM)
IN_SMEM = pl.BlockSpec(memory_space=pltpu.SMEM)


SMALL = pltpu.CompilerParams(vmem_limit_bytes=4 * 2**20)


def cost(rows, width):
    return pl.CostEstimate(flops=0, bytes_accessed=rows * width * 2, transcendentals=0)


def fetch(grad, table, parts, after, name):
    width = grad.shape[-1]
    sizes = [sum(n for _, _, _, n in part) for part in parts] * 2
    n_copies = 2 * sum(len(part) for part in parts)
    before = [] if after is None else [after]

    def kernel(table_ref, grad_ref, *refs):
        outs, sem = refs[len(before) : -1], refs[-1]
        copies = []
        for i, part in enumerate(parts * 2):
            other, row = int(i < len(parts)), 0
            for de, dy, first, n in part:
                copy = pltpu.make_async_copy(
                    grad_ref.at[pl.ds(block_row(table_ref, slot(de, dy, other), first), n)],
                    outs[i].at[pl.ds(row, n)],
                    sem.at[len(copies)],
                )
                copy.start()
                copies.append(copy)
                row += n
        for copy in copies:
            copy.wait()

    return pl.pallas_call(
        kernel,
        out_shape=[pltpu.VMEM((rows, width), jnp.bfloat16) for rows in sizes],
        in_specs=[IN_SMEM, IN_HBM] + [IN_VMEM] * len(before),
        out_specs=[IN_VMEM] * len(sizes),
        scratch_shapes=[pltpu.SemaphoreType.DMA((n_copies,))],
        compiler_params=SMALL,
        name=name,
        cost_estimate=cost(2 * sum(sizes), width),
    )(table, grad, *before)


def build(pieces, name, squares=False, after=()):
    arrays = list(after)
    for out in pieces:
        for _, sources in out:
            for x, _ in sources:
                if not any(x is have for have in arrays):
                    arrays.append(x)
    index = {id(x): i for i, x in enumerate(arrays)}
    plan = [[(n, [(index[id(x)], row) for x, row in sources]) for n, sources in out] for out in pieces]
    width = pieces[0][0][1][0][0].shape[-1]
    dtype = jnp.float32 if squares else jnp.bfloat16

    def kernel(*refs):
        ins, outs = refs[: len(arrays)], refs[len(arrays) :]
        total = None
        for out, out_ref in zip(plan, outs):
            at = 0
            for n, sources in out:
                for col in range(0, width, STEP_COLUMNS):
                    cols = pl.ds(col, STEP_COLUMNS)
                    terms = [ins[i][pl.ds(row, n), cols] for i, row in sources]
                    if len(terms) > 1:
                        acc = terms[0].astype(jnp.float32)
                        for term in terms[1:]:
                            acc += term.astype(jnp.float32)
                    else:
                        acc = terms[0]
                    out_ref[pl.ds(at, n), cols] = acc.astype(dtype)
                    if squares:
                        acc = acc * acc
                        for row in range(0, n, 8):
                            for lane in range(0, STEP_COLUMNS, 128):
                                part = acc[row : row + 8, lane : lane + 128]
                                total = part if total is None else total + part
                at += n
        if squares:
            outs[-1][...] = total

    shapes = [pltpu.VMEM((sum(n for n, _ in out), width), dtype) for out in plan]
    if squares:
        shapes.append(pltpu.VMEM((8, 128), jnp.float32))
    moved = sum(n * (1 + len(sources)) for out in plan for n, sources in out)
    return pl.pallas_call(
        kernel,
        out_shape=shapes,
        in_specs=[IN_VMEM] * len(arrays),
        out_specs=[IN_VMEM] * len(shapes),
        compiler_params=SMALL,
        name=name,
        cost_estimate=cost(moved, width),
    )(*arrays)


def place(out, table, pieces, name):
    arrays = []
    for x, *_ in pieces:
        if not any(x is have for have in arrays):
            arrays.append(x)
    index = {id(x): i for i, x in enumerate(arrays)}
    plan = [(index[id(x)], *rest) for x, *rest in pieces]
    width = arrays[0].shape[-1]
    old = [] if out is None else [out]

    def kernel(table_ref, *refs):
        ins, out_ref, token_ref, sem = refs[: len(arrays)], refs[-3], refs[-2], refs[-1]
        token_ref[...] = jnp.zeros_like(token_ref)
        copies = []
        for i, row, block, first, n in plan:
            copy = pltpu.make_async_copy(
                ins[i].at[pl.ds(row, n)],
                out_ref.at[pl.ds(block_row(table_ref, block, first), n)],
                sem.at[len(copies)],
            )
            copy.start()
            copies.append(copy)
        for copy in copies:
            copy.wait()

    return pl.pallas_call(
        kernel,
        out_shape=[
            jax.ShapeDtypeStruct((2048, width), jnp.bfloat16),
            pltpu.VMEM((8, 128), jnp.bfloat16),
        ],
        in_specs=[IN_SMEM] + [IN_VMEM] * len(arrays) + [IN_HBM] * len(old),
        out_specs=[IN_HBM, IN_VMEM],
        scratch_shapes=[pltpu.SemaphoreType.DMA((len(plan),))],
        input_output_aliases={1 + len(arrays): 0} if old else {},
        compiler_params=SMALL,
        name=name,
        cost_estimate=cost(2 * sum(p[-1] for p in plan), width),
    )(table, *arrays, *old)


def reduce_rows(grad, table):
    held = {}
    grad = pltpu.with_memory_space_constraint(grad, pltpu.HBM)

    def cross(parts, after, name):
        arrays = fetch(grad, table, parts, after, name)
        for k, part in enumerate(parts):
            got = to_other_core(arrays[k], f"{name}_{k}")
            row = 0
            for de, dy, first, n in part:
                for q in range(4):
                    if first <= START[q] < first + n:
                        at = row + START[q] - first
                        held[de, dy, q] = [(arrays[len(parts) + k], at), (got, at)]
                row += n

    cross(CORE_PARTS[0], None, "fetch0")
    for k, plan in enumerate(REDUCE):
        messages = build([[(SIZE[seg[2]], held[seg]) for seg in segs] for segs in plan.values()], f"sum{k}")
        if k == 0:
            cross(CORE_PARTS[1], messages[0], "fetch1")
        for (link, segs), x in zip(plan.items(), messages):
            at = layout(segs)
            got = send(link, x, f"reduce{k}")
            for seg in segs:
                held[over(link, seg)].append((got, at[seg]))

    return build([[(SIZE[seg[2]], held[seg]) for seg in OWN]], "own_sum", squares=True)


def runs_of(x, other, segs):
    runs = []
    for (de, dy, q), row in segs:
        last = runs[-1] if runs else None
        if last and last[1] == (de, dy) and last[2] + last[3] == START[q] and last[0] + last[3] == row:
            last[3] += SIZE[q]
        else:
            runs.append([row, (de, dy), START[q], SIZE[q]])
    pieces = []
    for row, (de, dy), first, n in runs:
        pieces.append((x, row, slot(de, dy, 0), first, n))
        pieces.append((other, row, slot(de, dy, 1), first, n))
    return pieces


def gather_rows(own, table):
    at = layout(OWN)
    held = {seg: (own, at[seg]) for seg in OWN}
    news, out, token = [(own, [(seg, at[seg]) for seg in OWN])], None, ()
    for k, plan in enumerate(GATHER):
        if k == 0:
            messages = [own] * len(plan)
        else:
            lists = plan.values()
            messages = build([[(SIZE[s[2]], [held[s]]) for s in segs] for segs in lists], f"copy{k}", after=token)
        came = []
        for (link, segs), x in zip(plan.items(), messages):
            at = layout(segs)
            got = send(link, x, f"gather{k}")
            came.append((got, [(over(link, seg), at[seg]) for seg in segs]))
        if k > 0:
            pieces = []
            for i, (x, segs) in enumerate(news):
                pieces.extend(runs_of(x, to_other_core(x, f"gather{k}_{i}"), segs))
            out, mark = place(out, table, pieces, f"place{k}")
            token = (mark,)
        for x, segs in came:
            held.update({seg: (x, row) for seg, row in segs})
        news = came if k > 0 else news + came
    last = sorted((seg for _, segs in news for seg, _ in segs), key=lambda seg: START[seg[2]])
    (x,) = build([[(SIZE[s[2]], [held[s]]) for s in last]], "copy3", after=token)
    at = layout(last)
    return place(out, table, runs_of(x, to_other_core(x, "last"), [(seg, at[seg]) for seg in last]), "place3")[0]


def total_over_all(x):
    x = jnp.sum(x, axis=0, keepdims=True)
    x = x + lax.ppermute(x, "dp_1", [(0, 1), (1, 0)])
    axes = ("ends", "dp_0", "tp_0", "tp_1")
    n = lax.axis_size(axes)
    return jnp.sum(lax.all_to_all(jnp.broadcast_to(x, (n, *x.shape)), axes, 0, 0))


def per_device(grad, master, moment, second):
    rows_tp = grad.shape[2]
    width = grad.shape[3]
    e, y, c = (lax.axis_index(a) for a in ENDS_DP)
    table = jnp.stack(
        [
            ((e ^ de) * 4 + (y ^ dy)) * 2 + (c ^ other)
            for de in range(2)
            for dy in range(4)
            for other in range(2)
        ]
    ).astype(jnp.int32)
    summed, parts = reduce_rows(grad.reshape(rows_tp, width), table)
    squares = total_over_all(parts)
    vocab_total = rows_tp * lax.axis_size(TP)
    factor = jnp.minimum(
        jnp.float32(1.0), jnp.sqrt(jnp.float32(vocab_total * width)) / (jnp.sqrt(squares) + 1e-06)
    )
    clipped = factor * summed
    moment_out = 0.9 * moment[0] + 0.1 * clipped
    second_out = 0.999 * second[0] + 0.001 * clipped * clipped
    update = moment_out / (1.0 - 0.9**STEP) / (jnp.sqrt(second_out / (1.0 - 0.999**STEP)) + 1e-08)
    master_out = master[0] - 0.01 * (update + 0.1 * master[0])
    weights = gather_rows(master_out.astype(jnp.bfloat16), table)
    return (weights, master_out[None], moment_out[None], second_out[None])


def solution(mesh):
    finer = Mesh(
        mesh.devices.reshape(mesh.shape["ends"], 4, 2, 2, 4),
        ("ends", "dp_0", "dp_1", "tp_0", "tp_1"),
    )
    return jax.shard_map(
        per_device,
        mesh=finer,
        in_specs=(
            P("ends", DP, TP, None),
            P(TP, ENDS_DP, None),
            P(TP, ENDS_DP, None),
            P(TP, ENDS_DP, None),
        ),
        out_specs=(P(TP, None), P(TP, ENDS_DP, None), P(TP, ENDS_DP, None), P(TP, ENDS_DP, None)),
        check_vma=False,
    )
```

```python
import jax
import jax.numpy as jnp
from jax import lax
from jax.experimental import pallas as pl
from jax.experimental.pallas import tpu as pltpu
from jax.sharding import Mesh
from jax.sharding import PartitionSpec as P

STEP = 10
ENDS_DP = ("ends", "dp_0", "dp_1")
TP = ("tp_0", "tp_1")
DP = ("dp_0", "dp_1")

SIZE = (32, 32, 32, 32)
START = (0, 64, 96, 32)
STEP_COLUMNS = 512
P1, P3, Z = "p1", "p3", "z"


def over(link, seg):
    de, dy, q = seg
    if link == P1:
        return (de, dy ^ 1, q)
    if link == P3:
        return (de, dy ^ 3, q)
    return (de ^ 1, dy, q)


REDUCE = (
    {
        Z: ((1, 2, 1), (1, 2, 2)),
        P1: ((1, 2, 0), (0, 2, 0)),
        P3: ((1, 2, 3), (0, 2, 3)),
    },
    {
        Z: ((1, 1, 1), (1, 3, 2)),
        P1: ((1, 1, 0), (0, 1, 0)),
        P3: ((1, 3, 3), (0, 3, 3)),
    },
    {
        Z: ((1, 3, 1), (1, 1, 2)),
        P1: ((0, 2, 1), (1, 1, 3)),
        P3: ((0, 2, 2), (1, 3, 0)),
    },
    {
        Z: ((1, 0, 1), (1, 0, 2)),
        P1: ((0, 1, 3), (0, 1, 1)),
        P3: ((0, 3, 0), (0, 3, 2)),
    },
    {
        Z: ((1, 0, 0), (1, 0, 3)),
        P1: ((0, 1, 2),),
        P3: ((0, 3, 1),),
    },
)
BUILT_TOGETHER = ((0, 1), (2,), (3,), (4,))
CORE_PARTS = (
    (
        (
            (1, 2, 0, 128),
            (0, 2, 0, 64),
            (1, 1, 0, 32),
            (1, 1, 64, 32),
            (1, 3, 32, 32),
            (1, 3, 96, 32),
            (0, 1, 0, 32),
            (0, 3, 32, 32),
        ),
    ),
    (
        ((1, 1, 32, 32), (1, 1, 96, 32), (1, 3, 0, 32), (1, 3, 64, 32), (0, 2, 64, 64)),
        ((1, 0, 0, 128), (0, 1, 32, 96), (0, 3, 0, 32), (0, 3, 64, 64)),
        ((0, 0, 0, 128),),
    ),
)
OWN = ((0, 0, 0), (0, 0, 3), (0, 0, 1), (0, 0, 2))
GATHER = (
    {Z: OWN, P1: OWN, P3: OWN},
    {
        Z: ((0, 3, 1), (0, 1, 1), (0, 1, 2), (0, 3, 2)),
        P1: ((1, 0, 0), (1, 0, 3), (0, 3, 0), (0, 3, 1)),
        P3: ((1, 0, 0), (1, 0, 3), (0, 1, 3), (0, 1, 2)),
    },
    {
        Z: ((0, 2, 1), (0, 2, 2)),
        P1: ((1, 3, 0),),
        P3: ((1, 1, 3),),
    },
)


def send(link, x, name):
    with jax.named_scope(f"{name}_{link}"):
        return _send(link, x)


def _send(link, x):
    if link == Z:
        return lax.ppermute(x, "ends", [(0, 1), (1, 0)])
    flip = 1 if link == P1 else 3
    return lax.ppermute(x, "dp_0", [(i, i ^ flip) for i in range(4)])


def to_other_core(x, name):
    with jax.named_scope(f"{name}_core"):
        return lax.ppermute(x, "dp_1", [(0, 1), (1, 0)])


def rows_of(segs):
    return sum(SIZE[q] for _, _, q in segs)


def layout(segs):
    at, row = {}, 0
    for seg in segs:
        at[seg] = row
        row += SIZE[seg[2]]
    return at


def slot(de, dy, other):
    return (de * 4 + dy) * 2 + other


def block_row(table, block, row):
    return pl.multiple_of(table[block] * 128 + row, 8)


IN_VMEM = pl.BlockSpec(memory_space=pltpu.VMEM)
IN_HBM = pl.BlockSpec(memory_space=pltpu.HBM)
IN_SMEM = pl.BlockSpec(memory_space=pltpu.SMEM)


SMALL = pltpu.CompilerParams(vmem_limit_bytes=4 * 2**20)


def cost(rows, width):
    return pl.CostEstimate(flops=0, bytes_accessed=rows * width * 2, transcendentals=0)


def fetch(grad, table, parts, other, after, name):
    width = grad.shape[-1]
    sizes = [sum(n for _, _, _, n in part) for part in parts]
    n_copies = sum(len(part) for part in parts)
    before = [] if after is None else [after]

    def kernel(table_ref, grad_ref, *refs):
        outs, sem = refs[len(before) : -1], refs[-1]
        copies = []
        for out, part in zip(outs, parts):
            row = 0
            for de, dy, first, n in part:
                copy = pltpu.make_async_copy(
                    grad_ref.at[pl.ds(block_row(table_ref, slot(de, dy, other), first), n)],
                    out.at[pl.ds(row, n)],
                    sem.at[len(copies)],
                )
                copy.start()
                copies.append(copy)
                row += n
        for copy in copies:
            copy.wait()

    return pl.pallas_call(
        kernel,
        out_shape=[pltpu.VMEM((rows, width), jnp.bfloat16) for rows in sizes],
        in_specs=[IN_SMEM, IN_HBM] + [IN_VMEM] * len(before),
        out_specs=[IN_VMEM] * len(sizes),
        scratch_shapes=[pltpu.SemaphoreType.DMA((n_copies,))],
        compiler_params=SMALL,
        name=name,
        cost_estimate=cost(2 * sum(sizes), width),
    )(table, grad, *before)


def build(pieces, name, squares=False, after=()):
    arrays = list(after)
    for out in pieces:
        for _, sources in out:
            for x, _ in sources:
                if not any(x is have for have in arrays):
                    arrays.append(x)
    index = {id(x): i for i, x in enumerate(arrays)}
    plan = [[(n, [(index[id(x)], row) for x, row in sources]) for n, sources in out] for out in pieces]
    width = pieces[0][0][1][0][0].shape[-1]
    dtype = jnp.float32 if squares else jnp.bfloat16

    def kernel(*refs):
        ins, outs = refs[: len(arrays)], refs[len(arrays) :]
        total = None
        for out, out_ref in zip(plan, outs):
            at = 0
            for n, sources in out:
                for col in range(0, width, STEP_COLUMNS):
                    cols = pl.ds(col, STEP_COLUMNS)
                    terms = [ins[i][pl.ds(row, n), cols] for i, row in sources]
                    if len(terms) > 1:
                        acc = terms[0].astype(jnp.float32)
                        for term in terms[1:]:
                            acc += term.astype(jnp.float32)
                    else:
                        acc = terms[0]
                    out_ref[pl.ds(at, n), cols] = acc.astype(dtype)
                    if squares:
                        acc = acc * acc
                        for row in range(0, n, 8):
                            for lane in range(0, STEP_COLUMNS, 128):
                                part = acc[row : row + 8, lane : lane + 128]
                                total = part if total is None else total + part
                at += n
        if squares:
            outs[-1][...] = total

    shapes = [pltpu.VMEM((sum(n for n, _ in out), width), dtype) for out in plan]
    if squares:
        shapes.append(pltpu.VMEM((8, 128), jnp.float32))
    moved = sum(n * (1 + len(sources)) for out in plan for n, sources in out)
    return pl.pallas_call(
        kernel,
        out_shape=shapes,
        in_specs=[IN_VMEM] * len(arrays),
        out_specs=[IN_VMEM] * len(shapes),
        compiler_params=SMALL,
        name=name,
        cost_estimate=cost(moved, width),
    )(*arrays)


def place(out, table, pieces, name):
    arrays = []
    for x, *_ in pieces:
        if not any(x is have for have in arrays):
            arrays.append(x)
    index = {id(x): i for i, x in enumerate(arrays)}
    plan = [(index[id(x)], *rest) for x, *rest in pieces]
    width = arrays[0].shape[-1]
    old = [] if out is None else [out]

    def kernel(table_ref, *refs):
        ins, out_ref, token_ref, sem = refs[: len(arrays)], refs[-3], refs[-2], refs[-1]
        token_ref[...] = jnp.zeros_like(token_ref)
        copies = []
        for i, row, block, first, n in plan:
            copy = pltpu.make_async_copy(
                ins[i].at[pl.ds(row, n)],
                out_ref.at[pl.ds(block_row(table_ref, block, first), n)],
                sem.at[len(copies)],
            )
            copy.start()
            copies.append(copy)
        for copy in copies:
            copy.wait()

    return pl.pallas_call(
        kernel,
        out_shape=[
            jax.ShapeDtypeStruct((2048, width), jnp.bfloat16),
            pltpu.VMEM((8, 128), jnp.bfloat16),
        ],
        in_specs=[IN_SMEM] + [IN_VMEM] * len(arrays) + [IN_HBM] * len(old),
        out_specs=[IN_HBM, IN_VMEM],
        scratch_shapes=[pltpu.SemaphoreType.DMA((len(plan),))],
        input_output_aliases={1 + len(arrays): 0} if old else {},
        compiler_params=SMALL,
        name=name,
        cost_estimate=cost(2 * sum(p[-1] for p in plan), width),
    )(table, *arrays, *old)


def reduce_rows(grad, table):
    held = {}
    grad = pltpu.with_memory_space_constraint(grad, pltpu.HBM)

    def cross(parts, others, owns, name):
        for k, (part, other, own) in enumerate(zip(parts, others, owns)):
            got = to_other_core(other, f"{name}_{k}")
            row = 0
            for de, dy, first, n in part:
                for q in range(4):
                    if first <= START[q] < first + n:
                        at = row + START[q] - first
                        held[de, dy, q] = [(own, at), (got, at)]
                row += n

    first, second = CORE_PARTS
    others = fetch(grad, table, first, 1, None, "fetch0")
    owns = fetch(grad, table, first, 0, others[0], "fetch1")
    cross(first, others, owns, "first")
    others = fetch(grad, table, second, 1, owns[0], "fetch2")
    for rounds in BUILT_TOGETHER:
        plan = [item for k in rounds for item in REDUCE[k].items()]
        lists = [[(SIZE[seg[2]], held[seg]) for seg in segs] for _, segs in plan]
        messages = build(lists, f"sum{rounds[0]}")
        if rounds[0] == 0:
            owns = fetch(grad, table, second, 0, messages[0], "fetch3")
            cross(second, others, owns, "second")
        for k, ((link, segs), x) in enumerate(zip(plan, messages)):
            at = layout(segs)
            got = send(link, x, f"reduce{rounds[k // 3]}")
            for seg in segs:
                held[over(link, seg)].append((got, at[seg]))

    return build([[(SIZE[seg[2]], held[seg]) for seg in OWN]], "own_sum", squares=True)


def runs_of(x, other, segs):
    runs = []
    for (de, dy, q), row in segs:
        last = runs[-1] if runs else None
        if last and last[1] == (de, dy) and last[2] + last[3] == START[q] and last[0] + last[3] == row:
            last[3] += SIZE[q]
        else:
            runs.append([row, (de, dy), START[q], SIZE[q]])
    pieces = []
    for row, (de, dy), first, n in runs:
        pieces.append((x, row, slot(de, dy, 0), first, n))
        pieces.append((other, row, slot(de, dy, 1), first, n))
    return pieces


def gather_rows(own, table):
    at = layout(OWN)
    held = {seg: (own, at[seg]) for seg in OWN}
    news, out, token = [(own, [(seg, at[seg]) for seg in OWN])], None, ()
    for k, plan in enumerate(GATHER):
        if k == 0:
            messages = [own] * len(plan)
        else:
            lists = plan.values()
            messages = build([[(SIZE[s[2]], [held[s]]) for s in segs] for segs in lists], f"copy{k}", after=[x for x, _ in news])
        came = []
        for (link, segs), x in zip(plan.items(), messages):
            at = layout(segs)
            got = send(link, x, f"gather{k}")
            came.append((got, [(over(link, seg), at[seg]) for seg in segs]))
        if k > 0:
            pieces = []
            for i, (x, segs) in enumerate(news):
                pieces.extend(runs_of(x, to_other_core(x, f"gather{k}_{i}"), segs))
            out, mark = place(out, table, pieces, f"place{k}")
            token = token or (mark,)
        for x, segs in came:
            held.update({seg: (x, row) for seg, row in segs})
        news = came if k > 0 else news + came
    last = sorted((seg for _, segs in news for seg, _ in segs), key=lambda seg: START[seg[2]])
    (x,) = build([[(SIZE[s[2]], [held[s]]) for s in last]], "copy3", after=token)
    at = layout(last)
    return place(out, table, runs_of(x, to_other_core(x, "last"), [(seg, at[seg]) for seg in last]), "place3")[0]


def total_over_all(x):
    x = jnp.sum(x, axis=0, keepdims=True)
    x = x + lax.ppermute(x, "dp_1", [(0, 1), (1, 0)])
    axes = ("ends", "dp_0", "tp_0", "tp_1")
    n = lax.axis_size(axes)
    return jnp.sum(lax.all_to_all(jnp.broadcast_to(x, (n, *x.shape)), axes, 0, 0))


def per_device(grad, master, moment, second):
    rows_tp = grad.shape[2]
    width = grad.shape[3]
    e, y, c = (lax.axis_index(a) for a in ENDS_DP)
    table = jnp.stack(
        [
            ((e ^ de) * 4 + (y ^ dy)) * 2 + (c ^ other)
            for de in range(2)
            for dy in range(4)
            for other in range(2)
        ]
    ).astype(jnp.int32)
    summed, parts = reduce_rows(grad.reshape(rows_tp, width), table)
    squares = total_over_all(parts)
    vocab_total = rows_tp * lax.axis_size(TP)
    factor = jnp.minimum(
        jnp.float32(1.0), jnp.sqrt(jnp.float32(vocab_total * width)) / (jnp.sqrt(squares) + 1e-06)
    )
    clipped = factor * summed
    moment_out = 0.9 * moment[0] + 0.1 * clipped
    second_out = 0.999 * second[0] + 0.001 * clipped * clipped
    update = moment_out / (1.0 - 0.9**STEP) / (jnp.sqrt(second_out / (1.0 - 0.999**STEP)) + 1e-08)
    master_out = master[0] - 0.01 * (update + 0.1 * master[0])
    weights = gather_rows(master_out.astype(jnp.bfloat16), table)
    return (weights, master_out[None], moment_out[None], second_out[None])


def solution(mesh):
    finer = Mesh(
        mesh.devices.reshape(mesh.shape["ends"], 4, 2, 2, 4),
        ("ends", "dp_0", "dp_1", "tp_0", "tp_1"),
    )
    return jax.shard_map(
        per_device,
        mesh=finer,
        in_specs=(
            P("ends", DP, TP, None),
            P(TP, ENDS_DP, None),
            P(TP, ENDS_DP, None),
            P(TP, ENDS_DP, None),
        ),
        out_specs=(P(TP, None), P(TP, ENDS_DP, None), P(TP, ENDS_DP, None), P(TP, ENDS_DP, None)),
        check_vma=False,
    )
```

```python
import jax
import jax.numpy as jnp
from jax import lax
from jax.experimental import pallas as pl
from jax.experimental.pallas import tpu as pltpu
from jax.sharding import Mesh
from jax.sharding import PartitionSpec as P

STEP = 10
ENDS_DP = ("ends", "dp_0", "dp_1")
TP = ("tp_0", "tp_1")
DP = ("dp_0", "dp_1")

SIZE = (32, 32, 32, 32)
START = (0, 64, 96, 32)
STEP_COLUMNS = 512
P1, P3, Z = "p1", "p3", "z"


def over(link, seg):
    de, dy, q = seg
    if link == P1:
        return (de, dy ^ 1, q)
    if link == P3:
        return (de, dy ^ 3, q)
    return (de ^ 1, dy, q)


REDUCE = (
    {
        Z: ((1, 2, 1), (1, 2, 2)),
        P1: ((1, 2, 0), (0, 2, 0)),
        P3: ((1, 2, 3), (0, 2, 3)),
    },
    {
        Z: ((1, 1, 1), (1, 3, 2)),
        P1: ((1, 1, 0), (0, 1, 0)),
        P3: ((1, 3, 3), (0, 3, 3)),
    },
    {
        Z: ((1, 3, 1), (1, 1, 2)),
        P1: ((0, 2, 1), (1, 1, 3)),
        P3: ((0, 2, 2), (1, 3, 0)),
    },
    {
        Z: ((1, 0, 1), (1, 0, 2)),
        P1: ((0, 1, 3), (0, 1, 1)),
        P3: ((0, 3, 0), (0, 3, 2)),
    },
    {
        Z: ((1, 0, 0), (1, 0, 3)),
        P1: ((0, 1, 2),),
        P3: ((0, 3, 1),),
    },
)
BUILT_TOGETHER = ((0, 1), (2,), (3,), (4,))
CORE_PARTS = (
    (
        (
            (1, 2, 0, 128),
            (0, 2, 0, 64),
            (1, 1, 0, 32),
            (1, 1, 64, 32),
            (1, 3, 32, 32),
            (1, 3, 96, 32),
            (0, 1, 0, 32),
            (0, 3, 32, 32),
        ),
    ),
    (
        ((1, 1, 32, 32), (1, 1, 96, 32), (1, 3, 0, 32), (1, 3, 64, 32), (0, 2, 64, 64)),
        ((1, 0, 0, 128), (0, 1, 32, 96), (0, 3, 0, 32), (0, 3, 64, 64)),
        ((0, 0, 0, 128),),
    ),
)
OWN = ((0, 0, 0), (0, 0, 3), (0, 0, 1), (0, 0, 2))
GATHER = (
    {Z: OWN, P1: OWN, P3: OWN},
    {
        Z: ((0, 3, 1), (0, 1, 1), (0, 1, 2), (0, 3, 2)),
        P1: ((1, 0, 0), (1, 0, 3), (0, 3, 0), (0, 3, 1)),
        P3: ((1, 0, 0), (1, 0, 3), (0, 1, 3), (0, 1, 2)),
    },
    {
        Z: ((0, 2, 1), (0, 2, 2)),
        P1: ((1, 3, 0),),
        P3: ((1, 1, 3),),
    },
)


def send(link, x, name):
    with jax.named_scope(f"{name}_{link}"):
        return _send(link, x)


def _send(link, x):
    if link == Z:
        return lax.ppermute(x, "ends", [(0, 1), (1, 0)])
    flip = 1 if link == P1 else 3
    return lax.ppermute(x, "dp_0", [(i, i ^ flip) for i in range(4)])


def to_other_core(x, name):
    with jax.named_scope(f"{name}_core"):
        return lax.ppermute(x, "dp_1", [(0, 1), (1, 0)])


def rows_of(segs):
    return sum(SIZE[q] for _, _, q in segs)


def layout(segs):
    at, row = {}, 0
    for seg in segs:
        at[seg] = row
        row += SIZE[seg[2]]
    return at


def slot(de, dy, other):
    return (de * 4 + dy) * 2 + other


def block_row(table, block, row):
    return pl.multiple_of(table[block] * 128 + row, 8)


IN_VMEM = pl.BlockSpec(memory_space=pltpu.VMEM)
IN_HBM = pl.BlockSpec(memory_space=pltpu.HBM)
IN_SMEM = pl.BlockSpec(memory_space=pltpu.SMEM)


SMALL = pltpu.CompilerParams(vmem_limit_bytes=4 * 2**20)


def cost(rows, width):
    return pl.CostEstimate(flops=0, bytes_accessed=rows * width * 2, transcendentals=0)


def fetch(grad, table, parts, other, after, name):
    width = grad.shape[-1]
    sizes = [sum(n for _, _, _, n in part) for part in parts]
    n_copies = sum(len(part) for part in parts)
    before = [] if after is None else [after]

    def kernel(table_ref, grad_ref, *refs):
        outs, sem = refs[len(before) : -1], refs[-1]
        copies = []
        for out, part in zip(outs, parts):
            row = 0
            for de, dy, first, n in part:
                copy = pltpu.make_async_copy(
                    grad_ref.at[pl.ds(block_row(table_ref, slot(de, dy, other), first), n)],
                    out.at[pl.ds(row, n)],
                    sem.at[len(copies)],
                )
                copy.start()
                copies.append(copy)
                row += n
        for copy in copies:
            copy.wait()

    return pl.pallas_call(
        kernel,
        out_shape=[pltpu.VMEM((rows, width), jnp.bfloat16) for rows in sizes],
        in_specs=[IN_SMEM, IN_HBM] + [IN_VMEM] * len(before),
        out_specs=[IN_VMEM] * len(sizes),
        scratch_shapes=[pltpu.SemaphoreType.DMA((n_copies,))],
        compiler_params=SMALL,
        name=name,
        cost_estimate=cost(2 * sum(sizes), width),
    )(table, grad, *before)


def build(pieces, name, squares=False, after=()):
    arrays = list(after)
    for out in pieces:
        for _, sources in out:
            for x, _ in sources:
                if not any(x is have for have in arrays):
                    arrays.append(x)
    index = {id(x): i for i, x in enumerate(arrays)}
    plan = [[(n, [(index[id(x)], row) for x, row in sources]) for n, sources in out] for out in pieces]
    width = pieces[0][0][1][0][0].shape[-1]
    dtype = jnp.float32 if squares else jnp.bfloat16

    def kernel(*refs):
        ins, outs = refs[: len(arrays)], refs[len(arrays) :]
        total, copies = None, []
        if squares:
            (sum_ref, square_ref, scratch, sem), outs = outs, outs[2:3]
        for out, out_ref in zip(plan, outs):
            at = 0
            for n, sources in out:
                for col in range(0, width, STEP_COLUMNS):
                    cols = pl.ds(col, STEP_COLUMNS)
                    terms = [ins[i][pl.ds(row, n), cols] for i, row in sources]
                    if len(terms) > 1:
                        acc = terms[0].astype(jnp.float32)
                        for term in terms[1:]:
                            acc += term.astype(jnp.float32)
                    else:
                        acc = terms[0]
                    out_ref[pl.ds(at, n), cols] = acc.astype(dtype)
                    if squares:
                        acc = acc * acc
                        for row in range(0, n, 8):
                            for lane in range(0, STEP_COLUMNS, 128):
                                part = acc[row : row + 8, lane : lane + 128]
                                total = part if total is None else total + part
                if squares:
                    some = pl.ds(at, n)
                    copies.append(pltpu.make_async_copy(scratch.at[some], sum_ref.at[some], sem.at[len(copies)]))
                    copies[-1].start()
                at += n
        if squares:
            square_ref[...] = total
        for copy in copies:
            copy.wait()

    shapes = [pltpu.VMEM((sum(n for n, _ in out), width), dtype) for out in plan]
    specs, scratch_shapes = [IN_VMEM] * len(shapes), []
    if squares:
        scratch_shapes = [shapes[0], pltpu.SemaphoreType.DMA((len(plan[0]),))]
        shapes = [pltpu.HBM(shapes[0].shape, dtype), pltpu.VMEM((8, 128), jnp.float32)]
        specs = [IN_HBM, IN_VMEM]
    moved = sum(n * (1 + len(sources)) for out in plan for n, sources in out)
    return pl.pallas_call(
        kernel,
        out_shape=shapes,
        in_specs=[IN_VMEM] * len(arrays),
        out_specs=specs,
        scratch_shapes=scratch_shapes,
        compiler_params=SMALL,
        name=name,
        cost_estimate=cost(moved, width),
    )(*arrays)


def place(out, table, pieces, name, stored=()):
    arrays = []
    for x, *_ in pieces:
        if not any(x is have for have in arrays):
            arrays.append(x)
    index = {id(x): i for i, x in enumerate(arrays)}
    plan = [(index[id(x)], *rest) for x, *rest in pieces]
    width = arrays[0].shape[-1]
    old = [] if out is None else [out]

    def kernel(table_ref, *refs):
        ins, sem = refs[: len(arrays)], refs[-1]
        stored_in = refs[len(arrays) : len(arrays) + len(stored)]
        out_ref, token_ref, *stored_out = refs[-3 - len(stored) : -1]
        token_ref[...] = jnp.zeros_like(token_ref)
        copies = []
        for x, to in zip(stored_in, stored_out):
            copy = pltpu.make_async_copy(x, to, sem.at[len(copies)])
            copy.start()
            copies.append(copy)
        for i, row, block, first, n in plan:
            copy = pltpu.make_async_copy(
                ins[i].at[pl.ds(row, n)],
                out_ref.at[pl.ds(block_row(table_ref, block, first), n)],
                sem.at[len(copies)],
            )
            copy.start()
            copies.append(copy)
        for copy in copies:
            copy.wait()

    return pl.pallas_call(
        kernel,
        out_shape=[
            jax.ShapeDtypeStruct((2048, width), jnp.bfloat16),
            pltpu.VMEM((8, 128), jnp.bfloat16),
            *(jax.ShapeDtypeStruct(x.shape, x.dtype) for x in stored),
        ],
        in_specs=[IN_SMEM] + [IN_VMEM] * (len(arrays) + len(stored)) + [IN_HBM] * len(old),
        out_specs=[IN_HBM, IN_VMEM] + [IN_HBM] * len(stored),
        scratch_shapes=[pltpu.SemaphoreType.DMA((len(plan) + len(stored),))],
        input_output_aliases={1 + len(arrays) + len(stored): 0} if old else {},
        compiler_params=SMALL,
        name=name,
        cost_estimate=cost(2 * sum(p[-1] for p in plan), width),
    )(table, *arrays, *stored, *old)


def reduce_rows(grad, table):
    held = {}
    grad = pltpu.with_memory_space_constraint(grad, pltpu.HBM)

    def cross(parts, others, owns, name):
        for k, (part, other, own) in enumerate(zip(parts, others, owns)):
            got = to_other_core(other, f"{name}_{k}")
            row = 0
            for de, dy, first, n in part:
                for q in range(4):
                    if first <= START[q] < first + n:
                        at = row + START[q] - first
                        held[de, dy, q] = [(own, at), (got, at)]
                row += n

    first, second = CORE_PARTS
    others = fetch(grad, table, first, 1, None, "fetch0")
    owns = fetch(grad, table, first, 0, others[0], "fetch1")
    cross(first, others, owns, "first")
    others = fetch(grad, table, second, 1, owns[0], "fetch2")
    for rounds in BUILT_TOGETHER:
        plan = [item for k in rounds for item in REDUCE[k].items()]
        lists = [[(SIZE[seg[2]], held[seg]) for seg in segs] for _, segs in plan]
        messages = build(lists, f"sum{rounds[0]}")
        if rounds[0] == 0:
            owns = fetch(grad, table, second, 0, messages[0], "fetch3")
            cross(second, others, owns, "second")
        for k, ((link, segs), x) in enumerate(zip(plan, messages)):
            at = layout(segs)
            got = send(link, x, f"reduce{rounds[k // 3]}")
            for seg in segs:
                held[over(link, seg)].append((got, at[seg]))

    return build([[(SIZE[seg[2]], held[seg]) for seg in OWN]], "own_sum", squares=True)


def runs_of(x, other, segs):
    runs = []
    for (de, dy, q), row in segs:
        last = runs[-1] if runs else None
        if last and last[1] == (de, dy) and last[2] + last[3] == START[q] and last[0] + last[3] == row:
            last[3] += SIZE[q]
        else:
            runs.append([row, (de, dy), START[q], SIZE[q]])
    pieces = []
    for row, (de, dy), first, n in runs:
        pieces.append((x, row, slot(de, dy, 0), first, n))
        pieces.append((other, row, slot(de, dy, 1), first, n))
    return pieces


def gather_rows(own, table, states):
    at = layout(OWN)
    held = {seg: (own, at[seg]) for seg in OWN}
    news, out, token, states_out = [(own, [(seg, at[seg]) for seg in OWN])], None, (), None
    for k, plan in enumerate(GATHER):
        if k == 0:
            messages = [own] * len(plan)
        else:
            lists = plan.values()
            messages = build([[(SIZE[s[2]], [held[s]]) for s in segs] for segs in lists], f"copy{k}", after=[x for x, _ in news])
        came = []
        for (link, segs), x in zip(plan.items(), messages):
            at = layout(segs)
            got = send(link, x, f"gather{k}")
            came.append((got, [(over(link, seg), at[seg]) for seg in segs]))
        if k > 0:
            pieces = []
            for i, (x, segs) in enumerate(news):
                pieces.extend(runs_of(x, to_other_core(x, f"gather{k}_{i}"), segs))
            out, mark, *stored = place(out, table, pieces, f"place{k}", states)
            states_out, states = states_out or stored, ()
            token = token or (mark,)
        for x, segs in came:
            held.update({seg: (x, row) for seg, row in segs})
        news = came if k > 0 else news + came
    last = sorted((seg for _, segs in news for seg, _ in segs), key=lambda seg: START[seg[2]])
    (x,) = build([[(SIZE[s[2]], [held[s]]) for s in last]], "copy3", after=token)
    at = layout(last)
    out, _ = place(out, table, runs_of(x, to_other_core(x, "last"), [(seg, at[seg]) for seg in last]), "place3")
    return out, states_out


def parts_of_total(x):
    x = jnp.sum(x, axis=0, keepdims=True)
    x = x + lax.ppermute(x, "dp_1", [(0, 1), (1, 0)])
    axes = ("ends", "dp_0", "tp_0", "tp_1")
    n = lax.axis_size(axes)
    return lax.all_to_all(jnp.broadcast_to(x, (n, *x.shape)), axes, 0, 0)


def adamw(parts, summed, master, moment, second, size):
    rows, width = summed.shape

    def kernel(parts_ref, *refs):
        from_hbm, (w_ref, master_out, moment_out, second_out) = refs[:4], refs[4:8]
        (summed_ref, master_ref, moment_ref, second_ref), sem = refs[8:12], refs[12]

        def load(k, i):
            at = pl.ds(k * 32, 32)
            return pltpu.make_async_copy(from_hbm[i].at[at], refs[8 + i].at[at], sem.at[k * 4 + i])

        for k in range(rows // 32):
            for i in range(4):
                load(k, i).start()
        squares = jnp.sum(jnp.sum(parts_ref[...], axis=0), axis=1, keepdims=True)
        limit = jnp.sqrt(jnp.full_like(squares, size))
        factor = jnp.minimum(1.0, limit / (jnp.sqrt(squares) + 1e-06))

        def some_rows(i, carry):
            at = pl.ds(pl.multiple_of(i * 16, 16), 16)
            for col in range(0, width, STEP_COLUMNS):
                cols = pl.ds(col, STEP_COLUMNS)
                clipped = factor * summed_ref[at, cols]
                m = 0.9 * moment_ref[at, cols] + 0.1 * clipped
                v = 0.999 * second_ref[at, cols] + 0.001 * clipped * clipped
                root = jnp.sqrt(v * (1.0 / (1.0 - 0.999**STEP))) + 1e-08
                update = m * (1.0 / (1.0 - 0.9**STEP)) / root
                old = master_ref[at, cols]
                new = old - 0.01 * (update + 0.1 * old)
                w_ref[at, cols] = new.astype(jnp.bfloat16)
                master_out[at, cols] = new
                moment_out[at, cols] = m
                second_out[at, cols] = v
            return carry

        for k in range(rows // 32):
            for i in range(4):
                load(k, i).wait()
            lax.fori_loop(2 * k, 2 * k + 2, some_rows, 0)

    return pl.pallas_call(
        kernel,
        out_shape=[pltpu.VMEM((rows, width), jnp.bfloat16)] + [pltpu.VMEM((rows, width), jnp.float32)] * 3,
        in_specs=[IN_VMEM] + [IN_HBM] * 4,
        out_specs=[IN_VMEM] * 4,
        scratch_shapes=[pltpu.VMEM((rows, width), jnp.float32)] * 4 + [pltpu.SemaphoreType.DMA((rows // 8,))],
        compiler_params=pltpu.CompilerParams(vmem_limit_bytes=10 * 2**20),
        name="adamw",
        cost_estimate=cost(15 * rows, width),
    )(parts, *(pltpu.with_memory_space_constraint(x, pltpu.HBM) for x in (summed, master, moment, second)))


def per_device(grad, master, moment, second):
    rows_tp = grad.shape[2]
    width = grad.shape[3]
    e, y, c = (lax.axis_index(a) for a in ENDS_DP)
    table = jnp.stack(
        [
            ((e ^ de) * 4 + (y ^ dy)) * 2 + (c ^ other)
            for de in range(2)
            for dy in range(4)
            for other in range(2)
        ]
    ).astype(jnp.int32)
    summed, parts = reduce_rows(grad.reshape(rows_tp, width), table)
    size = rows_tp * lax.axis_size(TP) * width
    rounded, *states = adamw(
        parts_of_total(parts), summed, master[0], moment[0], second[0], float(size)
    )
    weights, states = gather_rows(rounded, table, states)
    return (weights, *(x[None] for x in states))


def solution(mesh):
    finer = Mesh(
        mesh.devices.reshape(mesh.shape["ends"], 4, 2, 2, 4),
        ("ends", "dp_0", "dp_1", "tp_0", "tp_1"),
    )
    return jax.shard_map(
        per_device,
        mesh=finer,
        in_specs=(
            P("ends", DP, TP, None),
            P(TP, ENDS_DP, None),
            P(TP, ENDS_DP, None),
            P(TP, ENDS_DP, None),
        ),
        out_specs=(P(TP, None), P(TP, ENDS_DP, None), P(TP, ENDS_DP, None), P(TP, ENDS_DP, None)),
        check_vma=False,
    )
```

```python
import jax
import jax.numpy as jnp
from jax import lax
from jax.experimental import pallas as pl
from jax.experimental.pallas import tpu as pltpu
from jax.sharding import Mesh
from jax.sharding import PartitionSpec as P

STEP = 10
ENDS_DP = ("ends", "dp_0", "dp_1")
TP = ("tp_0", "tp_1")
DP = ("dp_0", "dp_1")

SIZE = (32, 32, 32, 32)
START = (0, 64, 96, 32)
STEP_COLUMNS = 512
P1, P3, Z = "p1", "p3", "z"


def over(link, seg):
    de, dy, q = seg
    if link == P1:
        return (de, dy ^ 1, q)
    if link == P3:
        return (de, dy ^ 3, q)
    return (de ^ 1, dy, q)


REDUCE = (
    {
        Z: ((1, 2, 1), (1, 2, 2)),
        P1: ((1, 2, 0), (0, 2, 0)),
        P3: ((1, 2, 3), (0, 2, 3)),
    },
    {
        Z: ((1, 1, 1), (1, 3, 2)),
        P1: ((1, 1, 0), (0, 1, 0)),
        P3: ((1, 3, 3), (0, 3, 3)),
    },
    {
        Z: ((1, 3, 1), (1, 1, 2)),
        P1: ((0, 2, 1), (1, 1, 3)),
        P3: ((0, 2, 2), (1, 3, 0)),
    },
    {
        Z: ((1, 0, 1), (1, 0, 2)),
        P1: ((0, 1, 3), (0, 1, 1)),
        P3: ((0, 3, 0), (0, 3, 2)),
    },
    {
        Z: ((1, 0, 0), (1, 0, 3)),
        P1: ((0, 1, 2),),
        P3: ((0, 3, 1),),
    },
)
BUILT_TOGETHER = ((0, 1), (2,), (3,), (4,))
CORE_PARTS = (
    (
        (
            (1, 2, 0, 128),
            (0, 2, 0, 64),
            (1, 1, 0, 32),
            (1, 1, 64, 32),
            (1, 3, 32, 32),
            (1, 3, 96, 32),
            (0, 1, 0, 32),
            (0, 3, 32, 32),
        ),
    ),
    (
        ((1, 1, 32, 32), (1, 1, 96, 32), (1, 3, 0, 32), (1, 3, 64, 32), (0, 2, 64, 64)),
        ((1, 0, 0, 128), (0, 1, 32, 96), (0, 3, 0, 32), (0, 3, 64, 64)),
        ((0, 0, 0, 128),),
    ),
)
OWN = ((0, 0, 0), (0, 0, 3), (0, 0, 1), (0, 0, 2))
GATHER = (
    {Z: OWN, P1: OWN, P3: OWN},
    {
        Z: ((0, 3, 1), (0, 1, 1), (0, 1, 2), (0, 3, 2)),
        P1: ((1, 0, 0), (1, 0, 3), (0, 3, 0), (0, 3, 1)),
        P3: ((1, 0, 0), (1, 0, 3), (0, 1, 3), (0, 1, 2)),
    },
    {
        Z: ((0, 2, 1), (0, 2, 2)),
        P1: ((1, 3, 0),),
        P3: ((1, 1, 3),),
    },
)


def send(link, x, name):
    with jax.named_scope(f"{name}_{link}"):
        return _send(link, x)


def _send(link, x):
    if link == Z:
        return lax.ppermute(x, "ends", [(0, 1), (1, 0)])
    flip = 1 if link == P1 else 3
    return lax.ppermute(x, "dp_0", [(i, i ^ flip) for i in range(4)])


def to_other_core(x, name):
    with jax.named_scope(f"{name}_core"):
        return lax.ppermute(x, "dp_1", [(0, 1), (1, 0)])


def rows_of(segs):
    return sum(SIZE[q] for _, _, q in segs)


def layout(segs):
    at, row = {}, 0
    for seg in segs:
        at[seg] = row
        row += SIZE[seg[2]]
    return at


def slot(de, dy, other):
    return (de * 4 + dy) * 2 + other


def block_row(table, block, row):
    return pl.multiple_of(table[block] * 128 + row, 8)


IN_VMEM = pl.BlockSpec(memory_space=pltpu.VMEM)
IN_HBM = pl.BlockSpec(memory_space=pltpu.HBM)
IN_SMEM = pl.BlockSpec(memory_space=pltpu.SMEM)


SMALL = pltpu.CompilerParams(vmem_limit_bytes=4 * 2**20)


def cost(rows, width):
    return pl.CostEstimate(flops=0, bytes_accessed=rows * width * 2, transcendentals=0)


def fetch(grad, table, parts, other, after, name):
    width = grad.shape[-1]
    sizes = [sum(n for _, _, _, n in part) for part in parts]
    n_copies = sum(len(part) for part in parts)
    before = [] if after is None else [after]

    def kernel(table_ref, grad_ref, *refs):
        outs, sem = refs[len(before) : -1], refs[-1]
        copies = []
        for out, part in zip(outs, parts):
            row = 0
            for de, dy, first, n in part:
                copy = pltpu.make_async_copy(
                    grad_ref.at[pl.ds(block_row(table_ref, slot(de, dy, other), first), n)],
                    out.at[pl.ds(row, n)],
                    sem.at[len(copies)],
                )
                copy.start()
                copies.append(copy)
                row += n
        for copy in copies:
            copy.wait()

    return pl.pallas_call(
        kernel,
        out_shape=[pltpu.VMEM((rows, width), jnp.bfloat16) for rows in sizes],
        in_specs=[IN_SMEM, IN_HBM] + [IN_VMEM] * len(before),
        out_specs=[IN_VMEM] * len(sizes),
        scratch_shapes=[pltpu.SemaphoreType.DMA((n_copies,))],
        compiler_params=SMALL,
        name=name,
        cost_estimate=cost(2 * sum(sizes), width),
    )(table, grad, *before)


def build(pieces, name, squares=False, after=()):
    arrays = list(after)
    for out in pieces:
        for _, sources in out:
            for x, _ in sources:
                if not any(x is have for have in arrays):
                    arrays.append(x)
    index = {id(x): i for i, x in enumerate(arrays)}
    plan = [[(n, [(index[id(x)], row) for x, row in sources]) for n, sources in out] for out in pieces]
    width = pieces[0][0][1][0][0].shape[-1]
    dtype = jnp.float32 if squares else jnp.bfloat16

    def kernel(*refs):
        ins, outs = refs[: len(arrays)], refs[len(arrays) :]
        total, copies = None, []
        if squares:
            (sum_ref, square_ref, scratch, sem), outs = outs, outs[2:3]
        for out, out_ref in zip(plan, outs):
            at = 0
            for n, sources in out:
                for col in range(0, width, STEP_COLUMNS):
                    cols = pl.ds(col, STEP_COLUMNS)
                    terms = [ins[i][pl.ds(row, n), cols] for i, row in sources]
                    if len(terms) > 1:
                        acc = terms[0].astype(jnp.float32)
                        for term in terms[1:]:
                            acc += term.astype(jnp.float32)
                    else:
                        acc = terms[0]
                    out_ref[pl.ds(at, n), cols] = acc.astype(dtype)
                    if squares:
                        acc = acc * acc
                        for row in range(0, n, 8):
                            for lane in range(0, STEP_COLUMNS, 128):
                                part = acc[row : row + 8, lane : lane + 128]
                                total = part if total is None else total + part
                if squares:
                    some = pl.ds(at, n)
                    copies.append(pltpu.make_async_copy(scratch.at[some], sum_ref.at[some], sem.at[len(copies)]))
                    copies[-1].start()
                at += n
        if squares:
            square_ref[...] = total
        for copy in copies:
            copy.wait()

    shapes = [pltpu.VMEM((sum(n for n, _ in out), width), dtype) for out in plan]
    specs, scratch_shapes = [IN_VMEM] * len(shapes), []
    if squares:
        scratch_shapes = [shapes[0], pltpu.SemaphoreType.DMA((len(plan[0]),))]
        shapes = [pltpu.HBM(shapes[0].shape, dtype), pltpu.VMEM((8, 128), jnp.float32)]
        specs = [IN_HBM, IN_VMEM]
    moved = sum(n * (1 + len(sources)) for out in plan for n, sources in out)
    return pl.pallas_call(
        kernel,
        out_shape=shapes,
        in_specs=[IN_VMEM] * len(arrays),
        out_specs=specs,
        scratch_shapes=scratch_shapes,
        compiler_params=SMALL,
        name=name,
        cost_estimate=cost(moved, width),
    )(*arrays)


def place(out, table, pieces, name, stored=()):
    arrays = []
    for x, *_ in pieces:
        if not any(x is have for have in arrays):
            arrays.append(x)
    index = {id(x): i for i, x in enumerate(arrays)}
    plan = [(index[id(x)], *rest) for x, *rest in pieces]
    width = arrays[0].shape[-1]
    old = [] if out is None else [out]

    def kernel(table_ref, *refs):
        ins, sem = refs[: len(arrays)], refs[-1]
        stored_in = refs[len(arrays) : len(arrays) + len(stored)]
        out_ref, token_ref, *stored_out = refs[-3 - len(stored) : -1]
        token_ref[...] = jnp.zeros_like(token_ref)
        copies = []
        for x, to in zip(stored_in, stored_out):
            copy = pltpu.make_async_copy(x, to, sem.at[len(copies)])
            copy.start()
            copies.append(copy)
        for i, row, block, first, n in plan:
            copy = pltpu.make_async_copy(
                ins[i].at[pl.ds(row, n)],
                out_ref.at[pl.ds(block_row(table_ref, block, first), n)],
                sem.at[len(copies)],
            )
            copy.start()
            copies.append(copy)
        for copy in copies:
            copy.wait()

    return pl.pallas_call(
        kernel,
        out_shape=[
            jax.ShapeDtypeStruct((2048, width), jnp.bfloat16),
            pltpu.VMEM((8, 128), jnp.bfloat16),
            *(jax.ShapeDtypeStruct(x.shape, x.dtype) for x in stored),
        ],
        in_specs=[IN_SMEM] + [IN_VMEM] * (len(arrays) + len(stored)) + [IN_HBM] * len(old),
        out_specs=[IN_HBM, IN_VMEM] + [IN_HBM] * len(stored),
        scratch_shapes=[pltpu.SemaphoreType.DMA((len(plan) + len(stored),))],
        input_output_aliases={1 + len(arrays) + len(stored): 0} if old else {},
        compiler_params=SMALL,
        name=name,
        cost_estimate=cost(2 * sum(p[-1] for p in plan), width),
    )(table, *arrays, *stored, *old)


def reduce_rows(grad, table):
    held = {}
    grad = pltpu.with_memory_space_constraint(grad, pltpu.HBM)

    def cross(parts, others, owns, name):
        for k, (part, other, own) in enumerate(zip(parts, others, owns)):
            got = to_other_core(other, f"{name}_{k}")
            row = 0
            for de, dy, first, n in part:
                for q in range(4):
                    if first <= START[q] < first + n:
                        at = row + START[q] - first
                        held[de, dy, q] = [(own, at), (got, at)]
                row += n

    first, second = CORE_PARTS
    others = fetch(grad, table, first, 1, None, "fetch0")
    owns = fetch(grad, table, first, 0, others[0], "fetch1")
    cross(first, others, owns, "first")
    others = fetch(grad, table, second, 1, owns[0], "fetch2")
    for rounds in BUILT_TOGETHER:
        plan = [item for k in rounds for item in REDUCE[k].items()]
        lists = [[(SIZE[seg[2]], held[seg]) for seg in segs] for _, segs in plan]
        messages = build(lists, f"sum{rounds[0]}")
        if rounds[0] == 0:
            owns = fetch(grad, table, second, 0, messages[0], "fetch3")
            cross(second, others, owns, "second")
        for k, ((link, segs), x) in enumerate(zip(plan, messages)):
            at = layout(segs)
            got = send(link, x, f"reduce{rounds[k // 3]}")
            for seg in segs:
                held[over(link, seg)].append((got, at[seg]))

    return build([[(SIZE[seg[2]], held[seg]) for seg in OWN]], "own_sum", squares=True)


def runs_of(x, other, segs):
    runs = []
    for (de, dy, q), row in segs:
        last = runs[-1] if runs else None
        if last and last[1] == (de, dy) and last[2] + last[3] == START[q] and last[0] + last[3] == row:
            last[3] += SIZE[q]
        else:
            runs.append([row, (de, dy), START[q], SIZE[q]])
    pieces = []
    for row, (de, dy), first, n in runs:
        pieces.append((x, row, slot(de, dy, 0), first, n))
        pieces.append((other, row, slot(de, dy, 1), first, n))
    return pieces


def gather_rows(own, table, states):
    at = layout(OWN)
    held = {seg: (own, at[seg]) for seg in OWN}
    news, out = [(own, [(seg, at[seg]) for seg in OWN])], None
    for k, plan in enumerate(GATHER):
        if k == 0:
            messages = [own] * len(plan)
        else:
            lists = plan.values()
            messages = build([[(SIZE[s[2]], [held[s]]) for s in segs] for segs in lists], f"copy{k}", after=[x for x, _ in news])
        came = []
        for (link, segs), x in zip(plan.items(), messages):
            at = layout(segs)
            got = send(link, x, f"gather{k}")
            came.append((got, [(over(link, seg), at[seg]) for seg in segs]))
        if k > 0:
            pieces = []
            for i, (x, segs) in enumerate(news):
                both = runs_of(x, to_other_core(x, f"gather{k}_{i}"), segs)
                pieces.extend(both if k == 1 else both[1::2])
            if k == 1:
                for x, segs in came:
                    pieces.extend(runs_of(x, x, segs)[::2])
                out, mark, *states = place(out, table, pieces, "place1", states)
        for x, segs in came:
            held.update({seg: (x, row) for seg, row in segs})
        news = came if k > 0 else news + came
    last = sorted((seg for _, segs in news for seg, _ in segs), key=lambda seg: START[seg[2]])
    (x,) = build([[(SIZE[s[2]], [held[s]]) for s in last]], "copy3", after=(mark,))
    at = layout(last)
    both = runs_of(x, to_other_core(x, "last"), [(seg, at[seg]) for seg in last])
    out, _ = place(out, table, pieces + both[::2], "place2")
    out, _ = place(out, table, both[1::2], "place3")
    return out, states


def parts_of_total(x):
    x = jnp.sum(x, axis=0, keepdims=True)
    x = x + lax.ppermute(x, "dp_1", [(0, 1), (1, 0)])
    axes = ("ends", "dp_0", "tp_0", "tp_1")
    n = lax.axis_size(axes)
    return lax.all_to_all(jnp.broadcast_to(x, (n, *x.shape)), axes, 0, 0)


def adamw(parts, summed, master, moment, second, size):
    rows, width = summed.shape

    def kernel(parts_ref, *refs):
        from_hbm, (w_ref, master_out, moment_out, second_out) = refs[:4], refs[4:8]
        (summed_ref, master_ref, moment_ref, second_ref), sem = refs[8:12], refs[12]

        def load(k, i):
            at = pl.ds(k * 32, 32)
            return pltpu.make_async_copy(from_hbm[i].at[at], refs[8 + i].at[at], sem.at[k * 4 + i])

        for k in range(rows // 32):
            for i in range(4):
                load(k, i).start()
        squares = jnp.sum(jnp.sum(parts_ref[...], axis=0), axis=1, keepdims=True)
        limit = jnp.sqrt(jnp.full_like(squares, size))
        factor = jnp.minimum(1.0, limit / (jnp.sqrt(squares) + 1e-06))

        def some_rows(i, carry):
            at = pl.ds(pl.multiple_of(i * 16, 16), 16)
            for col in range(0, width, STEP_COLUMNS):
                cols = pl.ds(col, STEP_COLUMNS)
                clipped = factor * summed_ref[at, cols]
                m = 0.9 * moment_ref[at, cols] + 0.1 * clipped
                v = 0.999 * second_ref[at, cols] + 0.001 * clipped * clipped
                root = jnp.sqrt(v * (1.0 / (1.0 - 0.999**STEP))) + 1e-08
                update = m * (1.0 / (1.0 - 0.9**STEP)) / root
                old = master_ref[at, cols]
                new = old - 0.01 * (update + 0.1 * old)
                w_ref[at, cols] = new.astype(jnp.bfloat16)
                master_out[at, cols] = new
                moment_out[at, cols] = m
                second_out[at, cols] = v
            return carry

        for k in range(rows // 32):
            for i in range(4):
                load(k, i).wait()
            lax.fori_loop(2 * k, 2 * k + 2, some_rows, 0)

    return pl.pallas_call(
        kernel,
        out_shape=[pltpu.VMEM((rows, width), jnp.bfloat16)] + [pltpu.VMEM((rows, width), jnp.float32)] * 3,
        in_specs=[IN_VMEM] + [IN_HBM] * 4,
        out_specs=[IN_VMEM] * 4,
        scratch_shapes=[pltpu.VMEM((rows, width), jnp.float32)] * 4 + [pltpu.SemaphoreType.DMA((rows // 8,))],
        compiler_params=pltpu.CompilerParams(vmem_limit_bytes=10 * 2**20),
        name="adamw",
        cost_estimate=cost(15 * rows, width),
    )(parts, *(pltpu.with_memory_space_constraint(x, pltpu.HBM) for x in (summed, master, moment, second)))


def per_device(grad, master, moment, second):
    rows_tp = grad.shape[2]
    width = grad.shape[3]
    e, y, c = (lax.axis_index(a) for a in ENDS_DP)
    table = jnp.stack(
        [
            ((e ^ de) * 4 + (y ^ dy)) * 2 + (c ^ other)
            for de in range(2)
            for dy in range(4)
            for other in range(2)
        ]
    ).astype(jnp.int32)
    summed, parts = reduce_rows(grad.reshape(rows_tp, width), table)
    size = rows_tp * lax.axis_size(TP) * width
    rounded, *states = adamw(
        parts_of_total(parts), summed, master[0], moment[0], second[0], float(size)
    )
    weights, states = gather_rows(rounded, table, states)
    return (weights, *(x[None] for x in states))


def solution(mesh):
    finer = Mesh(
        mesh.devices.reshape(mesh.shape["ends"], 4, 2, 2, 4),
        ("ends", "dp_0", "dp_1", "tp_0", "tp_1"),
    )
    return jax.shard_map(
        per_device,
        mesh=finer,
        in_specs=(
            P("ends", DP, TP, None),
            P(TP, ENDS_DP, None),
            P(TP, ENDS_DP, None),
            P(TP, ENDS_DP, None),
        ),
        out_specs=(P(TP, None), P(TP, ENDS_DP, None), P(TP, ENDS_DP, None), P(TP, ENDS_DP, None)),
        check_vma=False,
    )
```

```python
import jax
import jax.numpy as jnp
from jax import lax
from jax.experimental import pallas as pl
from jax.experimental.pallas import tpu as pltpu
from jax.sharding import Mesh
from jax.sharding import PartitionSpec as P

STEP = 10
ENDS_DP = ("ends", "dp_0", "dp_1")
TP = ("tp_0", "tp_1")
DP = ("dp_0", "dp_1")

SIZE = (32, 32, 32, 32)
START = (0, 64, 96, 32)
STEP_COLUMNS = 512
P1, P3, Z = "p1", "p3", "z"


def over(link, seg):
    de, dy, q = seg
    if link == P1:
        return (de, dy ^ 1, q)
    if link == P3:
        return (de, dy ^ 3, q)
    return (de ^ 1, dy, q)


REDUCE = (
    {
        Z: ((1, 2, 1), (1, 2, 2)),
        P1: ((1, 2, 0), (0, 2, 0)),
        P3: ((1, 2, 3), (0, 2, 3)),
    },
    {
        Z: ((1, 1, 1), (1, 3, 2)),
        P1: ((1, 1, 0), (0, 1, 0)),
        P3: ((1, 3, 3), (0, 3, 3)),
    },
    {
        Z: ((1, 3, 1), (1, 1, 2)),
        P1: ((0, 2, 1), (1, 1, 3)),
        P3: ((0, 2, 2), (1, 3, 0)),
    },
    {
        Z: ((1, 0, 1), (1, 0, 2)),
        P1: ((0, 1, 3), (0, 1, 1)),
        P3: ((0, 3, 0), (0, 3, 2)),
    },
    {
        Z: ((1, 0, 0), (1, 0, 3)),
        P1: ((0, 1, 2),),
        P3: ((0, 3, 1),),
    },
)
BUILT_TOGETHER = ((0, 1), (2,), (3,), (4,))
CORE_PARTS = (
    (
        (
            (1, 2, 0, 128),
            (0, 2, 0, 64),
            (1, 1, 0, 32),
            (1, 1, 64, 32),
            (1, 3, 32, 32),
            (1, 3, 96, 32),
            (0, 1, 0, 32),
            (0, 3, 32, 32),
        ),
    ),
    (
        ((1, 1, 32, 32), (1, 1, 96, 32), (1, 3, 0, 32), (1, 3, 64, 32), (0, 2, 64, 64)),
        ((1, 0, 0, 128), (0, 1, 32, 96), (0, 3, 0, 32), (0, 3, 64, 64)),
        ((0, 0, 0, 128),),
    ),
)
OWN = ((0, 0, 0), (0, 0, 3), (0, 0, 1), (0, 0, 2))
GATHER = (
    {Z: OWN, P1: OWN, P3: OWN},
    {
        Z: ((0, 3, 1), (0, 1, 1), (0, 1, 2), (0, 3, 2)),
        P1: ((1, 0, 0), (1, 0, 3), (0, 3, 0), (0, 3, 1)),
        P3: ((1, 0, 0), (1, 0, 3), (0, 1, 3), (0, 1, 2)),
    },
    {
        Z: ((0, 2, 1), (0, 2, 2)),
        P1: ((1, 3, 0),),
        P3: ((1, 1, 3),),
    },
)


def send(link, x, name):
    with jax.named_scope(f"{name}_{link}"):
        return _send(link, x)


def _send(link, x):
    if link == Z:
        return lax.ppermute(x, "ends", [(0, 1), (1, 0)])
    flip = 1 if link == P1 else 3
    return lax.ppermute(x, "dp_0", [(i, i ^ flip) for i in range(4)])


def to_other_core(x, name):
    with jax.named_scope(f"{name}_core"):
        return lax.ppermute(x, "dp_1", [(0, 1), (1, 0)])


def rows_of(segs):
    return sum(SIZE[q] for _, _, q in segs)


def layout(segs):
    at, row = {}, 0
    for seg in segs:
        at[seg] = row
        row += SIZE[seg[2]]
    return at


def slot(de, dy, other):
    return (de * 4 + dy) * 2 + other


def block_row(table, block, row):
    return pl.multiple_of(table[block] * 128 + row, 8)


IN_VMEM = pl.BlockSpec(memory_space=pltpu.VMEM)
IN_HBM = pl.BlockSpec(memory_space=pltpu.HBM)
IN_SMEM = pl.BlockSpec(memory_space=pltpu.SMEM)


SMALL = pltpu.CompilerParams(vmem_limit_bytes=4 * 2**20)


def cost(rows, width):
    return pl.CostEstimate(flops=0, bytes_accessed=rows * width * 2, transcendentals=0)


def fetch(grad, table, parts, other, after, name):
    width = grad.shape[-1]
    sizes = [sum(n for _, _, _, n in part) for part in parts]
    n_copies = sum(len(part) for part in parts)
    before = [] if after is None else [after]

    def kernel(table_ref, grad_ref, *refs):
        outs, sem = refs[len(before) : -1], refs[-1]
        copies = []
        for out, part in zip(outs, parts):
            row = 0
            for de, dy, first, n in part:
                copy = pltpu.make_async_copy(
                    grad_ref.at[pl.ds(block_row(table_ref, slot(de, dy, other), first), n)],
                    out.at[pl.ds(row, n)],
                    sem.at[len(copies)],
                )
                copy.start()
                copies.append(copy)
                row += n
        for copy in copies:
            copy.wait()

    return pl.pallas_call(
        kernel,
        out_shape=[pltpu.VMEM((rows, width), jnp.bfloat16) for rows in sizes],
        in_specs=[IN_SMEM, IN_HBM] + [IN_VMEM] * len(before),
        out_specs=[IN_VMEM] * len(sizes),
        scratch_shapes=[pltpu.SemaphoreType.DMA((n_copies,))],
        compiler_params=SMALL,
        name=name,
        cost_estimate=cost(2 * sum(sizes), width),
    )(table, grad, *before)


def build(pieces, name, squares=False, after=()):
    arrays = list(after)
    for out in pieces:
        for _, sources in out:
            for x, _ in sources:
                if not any(x is have for have in arrays):
                    arrays.append(x)
    index = {id(x): i for i, x in enumerate(arrays)}
    plan = [[(n, [(index[id(x)], row) for x, row in sources]) for n, sources in out] for out in pieces]
    width = pieces[0][0][1][0][0].shape[-1]
    dtype = jnp.float32 if squares else jnp.bfloat16

    def kernel(*refs):
        ins, outs = refs[: len(arrays)], refs[len(arrays) :]
        total, copies = None, []
        if squares:
            (sum_ref, square_ref, scratch, sem), outs = outs, outs[2:3]
        for out, out_ref in zip(plan, outs):
            at = 0
            for n, sources in out:
                for col in range(0, width, STEP_COLUMNS):
                    cols = pl.ds(col, STEP_COLUMNS)
                    terms = [ins[i][pl.ds(row, n), cols] for i, row in sources]
                    if len(terms) > 1:
                        acc = terms[0].astype(jnp.float32)
                        for term in terms[1:]:
                            acc += term.astype(jnp.float32)
                    else:
                        acc = terms[0]
                    out_ref[pl.ds(at, n), cols] = acc.astype(dtype)
                    if squares:
                        acc = acc * acc
                        for row in range(0, n, 8):
                            for lane in range(0, STEP_COLUMNS, 128):
                                part = acc[row : row + 8, lane : lane + 128]
                                total = part if total is None else total + part
                if squares:
                    some = pl.ds(at, n)
                    copies.append(pltpu.make_async_copy(scratch.at[some], sum_ref.at[some], sem.at[len(copies)]))
                    copies[-1].start()
                at += n
        if squares:
            square_ref[...] = total
        for copy in copies:
            copy.wait()

    shapes = [pltpu.VMEM((sum(n for n, _ in out), width), dtype) for out in plan]
    specs, scratch_shapes = [IN_VMEM] * len(shapes), []
    if squares:
        scratch_shapes = [shapes[0], pltpu.SemaphoreType.DMA((len(plan[0]),))]
        shapes = [pltpu.HBM(shapes[0].shape, dtype), pltpu.VMEM((8, 128), jnp.float32)]
        specs = [IN_HBM, IN_VMEM]
    moved = sum(n * (1 + len(sources)) for out in plan for n, sources in out)
    return pl.pallas_call(
        kernel,
        out_shape=shapes,
        in_specs=[IN_VMEM] * len(arrays),
        out_specs=specs,
        scratch_shapes=scratch_shapes,
        compiler_params=SMALL,
        name=name,
        cost_estimate=cost(moved, width),
    )(*arrays)


def place(out, table, pieces, name, stored=()):
    arrays = []
    for x, *_ in pieces:
        if not any(x is have for have in arrays):
            arrays.append(x)
    index = {id(x): i for i, x in enumerate(arrays)}
    plan = [(index[id(x)], *rest) for x, *rest in pieces]
    width = arrays[0].shape[-1]
    old = [] if out is None else [out]

    def kernel(table_ref, *refs):
        ins, sem = refs[: len(arrays)], refs[-1]
        stored_in = refs[len(arrays) : len(arrays) + len(stored)]
        out_ref, token_ref, *stored_out = refs[-3 - len(stored) : -1]
        token_ref[...] = jnp.zeros_like(token_ref)
        copies = []
        for x, to in zip(stored_in, stored_out):
            copy = pltpu.make_async_copy(x, to, sem.at[len(copies)])
            copy.start()
            copies.append(copy)
        for i, row, block, first, n in plan:
            copy = pltpu.make_async_copy(
                ins[i].at[pl.ds(row, n)],
                out_ref.at[pl.ds(block_row(table_ref, block, first), n)],
                sem.at[len(copies)],
            )
            copy.start()
            copies.append(copy)
        for copy in copies:
            copy.wait()

    return pl.pallas_call(
        kernel,
        out_shape=[
            jax.ShapeDtypeStruct((2048, width), jnp.bfloat16),
            pltpu.VMEM((8, 128), jnp.bfloat16),
            *(jax.ShapeDtypeStruct(x.shape, x.dtype) for x in stored),
        ],
        in_specs=[IN_SMEM] + [IN_VMEM] * (len(arrays) + len(stored)) + [IN_HBM] * len(old),
        out_specs=[IN_HBM, IN_VMEM] + [IN_HBM] * len(stored),
        scratch_shapes=[pltpu.SemaphoreType.DMA((len(plan) + len(stored),))],
        input_output_aliases={1 + len(arrays) + len(stored): 0} if old else {},
        compiler_params=SMALL,
        name=name,
        cost_estimate=cost(2 * sum(p[-1] for p in plan), width),
    )(table, *arrays, *stored, *old)


def reduce_rows(grad, table):
    held = {}
    grad = pltpu.with_memory_space_constraint(grad, pltpu.HBM)

    def cross(parts, others, owns, name):
        for k, (part, other, own) in enumerate(zip(parts, others, owns)):
            got = to_other_core(other, f"{name}_{k}")
            row = 0
            for de, dy, first, n in part:
                for q in range(4):
                    if first <= START[q] < first + n:
                        at = row + START[q] - first
                        held[de, dy, q] = [(own, at), (got, at)]
                row += n

    first, second = CORE_PARTS
    others = fetch(grad, table, first, 1, None, "fetch0")
    owns = fetch(grad, table, first, 0, others[0], "fetch1")
    cross(first, others, owns, "first")
    others = fetch(grad, table, second[:-1], 1, owns[0], "fetch2")
    for rounds in BUILT_TOGETHER:
        plan = [item for k in rounds for item in REDUCE[k].items()]
        lists = [[(SIZE[seg[2]], held[seg]) for seg in segs] for _, segs in plan]
        messages = build(lists, f"sum{rounds[0]}")
        if rounds[0] == 0:
            owns = fetch(grad, table, second, 0, messages[0], "fetch3")
            others += fetch(grad, table, second[-1:], 1, owns[0], "fetch4")
            cross(second, others, owns, "second")
        for k, ((link, segs), x) in enumerate(zip(plan, messages)):
            at = layout(segs)
            got = send(link, x, f"reduce{rounds[k // 3]}")
            for seg in segs:
                held[over(link, seg)].append((got, at[seg]))

    return build([[(SIZE[seg[2]], held[seg]) for seg in OWN]], "own_sum", squares=True)


def runs_of(x, other, segs):
    runs = []
    for (de, dy, q), row in segs:
        last = runs[-1] if runs else None
        if last and last[1] == (de, dy) and last[2] + last[3] == START[q] and last[0] + last[3] == row:
            last[3] += SIZE[q]
        else:
            runs.append([row, (de, dy), START[q], SIZE[q]])
    pieces = []
    for row, (de, dy), first, n in runs:
        pieces.append((x, row, slot(de, dy, 0), first, n))
        pieces.append((other, row, slot(de, dy, 1), first, n))
    return pieces


def gather_rows(own, table, states):
    at = layout(OWN)
    held = {seg: (own, at[seg]) for seg in OWN}
    news, out = [(own, [(seg, at[seg]) for seg in OWN])], None
    for k, plan in enumerate(GATHER):
        if k == 0:
            messages = [own] * len(plan)
        else:
            lists = plan.values()
            messages = build([[(SIZE[s[2]], [held[s]]) for s in segs] for segs in lists], f"copy{k}", after=[x for x, _ in news])
        came = []
        for (link, segs), x in zip(plan.items(), messages):
            at = layout(segs)
            got = send(link, x, f"gather{k}")
            came.append((got, [(over(link, seg), at[seg]) for seg in segs]))
        if k > 0:
            pieces = []
            for i, (x, segs) in enumerate(news):
                both = runs_of(x, to_other_core(x, f"gather{k}_{i}"), segs)
                pieces.extend(both if k == 1 else both[1::2])
            if k == 1:
                for x, segs in came:
                    pieces.extend(runs_of(x, x, segs)[::2])
                out, mark, *states = place(out, table, pieces, "place1", states)
        for x, segs in came:
            held.update({seg: (x, row) for seg, row in segs})
        news = came if k > 0 else news + came
    last = sorted((seg for _, segs in news for seg, _ in segs), key=lambda seg: START[seg[2]])
    (x,) = build([[(SIZE[s[2]], [held[s]]) for s in last]], "copy3", after=(mark,))
    at = layout(last)
    both = runs_of(x, to_other_core(x, "last"), [(seg, at[seg]) for seg in last])
    out, _ = place(out, table, pieces + both[::2], "place2")
    out, _ = place(out, table, both[1::2], "place3")
    return out, states


def parts_of_total(x):
    x = jnp.sum(x, axis=0, keepdims=True)
    x = x + lax.ppermute(x, "dp_1", [(0, 1), (1, 0)])
    axes = ("ends", "dp_0", "tp_0", "tp_1")
    n = lax.axis_size(axes)
    return lax.all_to_all(jnp.broadcast_to(x, (n, *x.shape)), axes, 0, 0)


def adamw(parts, summed, master, moment, second, size):
    rows, width = summed.shape

    def kernel(parts_ref, *refs):
        from_hbm, (w_ref, master_out, moment_out, second_out) = refs[:4], refs[4:8]
        (summed_ref, master_ref, moment_ref, second_ref), sem = refs[8:12], refs[12]

        def load(k, i):
            at = pl.ds(k * 32, 32)
            return pltpu.make_async_copy(from_hbm[i].at[at], refs[8 + i].at[at], sem.at[k * 4 + i])

        for k in range(rows // 32):
            for i in range(4):
                load(k, i).start()
        squares = jnp.sum(jnp.sum(parts_ref[...], axis=0), axis=1, keepdims=True)
        limit = jnp.sqrt(jnp.full_like(squares, size))
        factor = jnp.minimum(1.0, limit / (jnp.sqrt(squares) + 1e-06))

        def some_rows(i, carry):
            at = pl.ds(pl.multiple_of(i * 16, 16), 16)
            for col in range(0, width, STEP_COLUMNS):
                cols = pl.ds(col, STEP_COLUMNS)
                clipped = factor * summed_ref[at, cols]
                m = 0.9 * moment_ref[at, cols] + 0.1 * clipped
                v = 0.999 * second_ref[at, cols] + 0.001 * clipped * clipped
                root = jnp.sqrt(v * (1.0 / (1.0 - 0.999**STEP))) + 1e-08
                update = m * (1.0 / (1.0 - 0.9**STEP)) / root
                old = master_ref[at, cols]
                new = old - 0.01 * (update + 0.1 * old)
                w_ref[at, cols] = new.astype(jnp.bfloat16)
                master_out[at, cols] = new
                moment_out[at, cols] = m
                second_out[at, cols] = v
            return carry

        for k in range(rows // 32):
            for i in range(4):
                load(k, i).wait()
            lax.fori_loop(2 * k, 2 * k + 2, some_rows, 0)

    return pl.pallas_call(
        kernel,
        out_shape=[pltpu.VMEM((rows, width), jnp.bfloat16)] + [pltpu.VMEM((rows, width), jnp.float32)] * 3,
        in_specs=[IN_VMEM] + [IN_HBM] * 4,
        out_specs=[IN_VMEM] * 4,
        scratch_shapes=[pltpu.VMEM((rows, width), jnp.float32)] * 4 + [pltpu.SemaphoreType.DMA((rows // 8,))],
        compiler_params=pltpu.CompilerParams(vmem_limit_bytes=10 * 2**20),
        name="adamw",
        cost_estimate=cost(15 * rows, width),
    )(parts, *(pltpu.with_memory_space_constraint(x, pltpu.HBM) for x in (summed, master, moment, second)))


def per_device(grad, master, moment, second):
    rows_tp = grad.shape[2]
    width = grad.shape[3]
    e, y, c = (lax.axis_index(a) for a in ENDS_DP)
    table = jnp.stack(
        [
            ((e ^ de) * 4 + (y ^ dy)) * 2 + (c ^ other)
            for de in range(2)
            for dy in range(4)
            for other in range(2)
        ]
    ).astype(jnp.int32)
    summed, parts = reduce_rows(grad.reshape(rows_tp, width), table)
    size = rows_tp * lax.axis_size(TP) * width
    rounded, *states = adamw(
        parts_of_total(parts), summed, master[0], moment[0], second[0], float(size)
    )
    weights, states = gather_rows(rounded, table, states)
    return (weights, *(x[None] for x in states))


def solution(mesh):
    finer = Mesh(
        mesh.devices.reshape(mesh.shape["ends"], 4, 2, 2, 4),
        ("ends", "dp_0", "dp_1", "tp_0", "tp_1"),
    )
    return jax.shard_map(
        per_device,
        mesh=finer,
        in_specs=(
            P("ends", DP, TP, None),
            P(TP, ENDS_DP, None),
            P(TP, ENDS_DP, None),
            P(TP, ENDS_DP, None),
        ),
        out_specs=(P(TP, None), P(TP, ENDS_DP, None), P(TP, ENDS_DP, None), P(TP, ENDS_DP, None)),
        check_vma=False,
    )
```
